512 devices in a mesh: net: 16 (over z), seg: 8 (over y, core), corner: 4 (over x).
Axes of the slice: x: 4, y: 4, z: 16, core: 2. Of those that a mesh axis runs over, the one named last changes fastest.
Arguments:
- tile_values: bfloat16 [8192, 128, 1024], P(('net', 'seg', 'corner')), may hold values from -48 to 48
- tile_coords: int32 [8192, 3], P(('net', 'seg', 'corner')), may hold values from 0 to 511, as said below
- tile_count: int32 [512], P(('net', 'seg', 'corner')), may hold values from 12 to 16, as said below
- owner_map: int32 [512], P('net'), may hold values from 0 to 511, as said below
- corner_factor: bfloat16 [64, 256], P('corner')
- seg_factor: bfloat16 [65536, 256], P(('seg', 'net'))
Outputs:
- net_factor: float32 [65536, 256], P(('net', 'seg', 'corner'))
The draws below stay inside these ranges and needn't reach their ends.
Inputs may be any that keep to these rules, and one draw needn't show every extreme that they name: `tile_coords`: row t of device d gives a corner block within the corner range stored by d's corner index, a net block that owner_map assigns to an owner slot of d's net index, and a segment block within the segment range of d's seg index. Among a device's 16 rows at most 2 name segment blocks stored by any one device of the net axis, and on every device two live rows name segment blocks stored by the same device of the net axis. The first tile_count[d] rows of device d are live; the others are ignored. `owner_map`: A permutation of the 512 net blocks.
All inputs are finite; a program needn't handle non-finite values.
Results may differ from the reference program's by a relative error of at most 0.0058.
The reference program's roundings to bfloat16 on the way (of `khatri`) count: a program that leaves them out, or rounds other values in their place, can miss the bound.
Values may be sent and summed in bfloat16 or wider, within the bound.
No kernel may reach another device: no remote copies, remote signals or barrier semaphores. Data moves between devices by JAX's collectives and lax.ppermute only.
A program may use at most 64 MiB of HBM per device.

```python
import math
import jax
import jax.numpy as jnp
from jax import lax

R = 256
CORNERS = 64
CBLK = 8
NETB = 128
SEGB = 128
TILES_DEV = 16
BPH = 4
CAP = 2
GROUP = 32
NBLK = 512
SEGS = 65536
N_NET = 16
N_SEG = 8
N_CORNER = 4


def layout(key):
    key_owner, key_count, key_full, key_chosen, key_devices = jax.random.split(key, 5)
    owners = jax.random.permutation(key_owner, NBLK).astype(jnp.int32)
    device_ids = jnp.arange(NBLK, dtype=jnp.int32)
    lowest = max(2, 3 * TILES_DEV // 4)
    highest = max(lowest, TILES_DEV)
    counts = jax.random.randint(key_count, (NBLK,), lowest, highest + 1)
    heavy = jax.random.randint(key_full, (NBLK,), 0, 8) == 0
    chosen = jax.random.randint(key_chosen, (), 0, NBLK)
    light = (chosen + 1) % NBLK
    counts = jnp.where(heavy | (device_ids == chosen), TILES_DEV, counts)
    counts = jnp.where(device_ids == light, lowest, counts).astype(jnp.int32)
    corner_span = CORNERS // CBLK // N_CORNER

    def device_tiles(device_key, device, count):
        net_index = device // GROUP
        seg_index = device // N_CORNER % N_SEG
        corner_index = device % N_CORNER
        key_corner, key_net, key_slots, key_within, key_order = jax.random.split(device_key, 5)
        corner = corner_index * corner_span + jax.random.randint(key_corner, (TILES_DEV,), 0, corner_span)
        net_block = owners[net_index * GROUP + jax.random.randint(key_net, (TILES_DEV,), 0, GROUP)]
        slots = jax.random.permutation(key_slots, N_NET * CAP).astype(jnp.int32)
        partner = jnp.bitwise_xor(slots[0], 1)
        positions = jnp.arange(N_NET * CAP, dtype=jnp.int32)
        sort_keys = jnp.where(slots == partner, 1, 2 * positions)
        ordered = slots[jnp.argsort(sort_keys, stable=True)][:TILES_DEV]
        holder = ordered // CAP
        within = jax.random.randint(key_within, (TILES_DEV,), 0, BPH)
        segment = seg_index * BPH * N_NET + holder * BPH + within
        tile_ids = jnp.arange(TILES_DEV, dtype=jnp.int32)
        shuffle = jax.random.permutation(key_order, TILES_DEV).astype(jnp.int32)
        order_keys = jnp.where(tile_ids < count, shuffle, TILES_DEV + tile_ids)
        order = jnp.argsort(order_keys, stable=True)
        coords = jnp.stack([corner, net_block, segment], axis=1).astype(jnp.int32)
        return coords[order]
    device_keys = jax.vmap(lambda device: jax.random.fold_in(key_devices, device))(device_ids)
    coords = jax.vmap(device_tiles)(device_keys, device_ids, counts)
    return (owners, counts, coords.reshape(NBLK * TILES_DEV, 3))


def draw_tile_coords(key, part):
    owners, counts, coords = layout(jax.random.fold_in(key, 11))
    return coords


def draw_tile_count(key, part):
    owners, counts, coords = layout(jax.random.fold_in(key, 11))
    return counts


def draw_owner_map(key, part):
    owners, counts, coords = layout(jax.random.fold_in(key, 11))
    return owners


def draw_corner_factor(key, part):
    key_rows, key_base, key_cols = jax.random.split(key, 3)
    row_pos = jnp.arange(CORNERS, dtype=jnp.float32) / (CORNERS - 1)
    rising = (1.0 + 2.0 * row_pos)[:, None]
    spread = jnp.exp(jax.random.uniform(key_rows, (CORNERS, 1), minval=0.0, maxval=math.log(10.0)))
    base = jax.random.normal(key_base, (CORNERS, R))
    cols = jnp.exp(jax.random.uniform(key_cols, (1, R), minval=0.0, maxval=math.log(2.0)))
    scaled = base * spread * rising * cols / math.sqrt(CORNERS * 30.0)
    return scaled.astype(jnp.bfloat16)


def draw_seg_factor(key, part):
    key_rows, key_base, key_cols = jax.random.split(key, 3)
    row_pos = jnp.arange(SEGS, dtype=jnp.float32) / (SEGS - 1)
    rising = (1.0 + 2.0 * row_pos)[:, None]
    spread = jnp.exp(jax.random.uniform(key_rows, (SEGS, 1), minval=0.0, maxval=math.log(10.0)))
    base = jax.random.uniform(key_base, (SEGS, R), minval=0.2, maxval=1.0)
    cols = jnp.exp(jax.random.uniform(key_cols, (1, R), minval=0.0, maxval=math.log(2.0)))
    scaled = base * spread * rising * cols / math.sqrt(SEGS * 30.0)
    return scaled.astype(jnp.bfloat16)


def levels(stream_key, shape, cuts, smallest, largest):
    factor_of = 1.0
    for axis_at, blocks in cuts:
        steps = jax.random.uniform(jax.random.fold_in(jax.random.fold_in(stream_key, 6), axis_at), (blocks,), jnp.float32, smallest / len(cuts), largest / len(cuts))
        factor_of = factor_of * jnp.repeat(jnp.exp(steps), shape[axis_at] // blocks).reshape((-1,) + (1,) * (len(shape) - 1 - axis_at))
    return factor_of


def bell_draw(stream_key, dims, width, bound, pieces=(), kind=jnp.bfloat16):
    level = levels(stream_key, dims, pieces, -0.22, 0.18) if pieces else 1.0
    entries = jax.random.normal(stream_key, dims, jnp.float32) * width * level
    return jnp.minimum(jnp.maximum(entries, -bound), bound).astype(kind)


def setup_inputs(seed: int = 0) -> dict:
    key_of = jax.random.split(jax.random.key(seed), 7)
    tile_values = bell_draw(key_of[0], (NBLK * TILES_DEV, NETB, CBLK * SEGB), 8.0, 48.0, ((0, 512),))
    tile_coords = draw_tile_coords(jax.random.fold_in(key_of[6], 71), 0)
    tile_count = draw_tile_count(jax.random.fold_in(key_of[6], 71), 0)
    owner_map = draw_owner_map(jax.random.fold_in(key_of[6], 71), 0)
    corner_factor = draw_corner_factor(jax.random.fold_in(key_of[6], 71), 0)
    seg_factor = draw_seg_factor(jax.random.fold_in(key_of[6], 71), 0)
    return {"tile_values": tile_values, "tile_coords": tile_coords, "tile_count": tile_count, "owner_map": owner_map, "corner_factor": corner_factor, "seg_factor": seg_factor}


def solve_rows(gram, mttkrp):
    cholesky_low = jnp.linalg.cholesky(gram)
    forward = lax.linalg.triangular_solve(cholesky_low, mttkrp.T, left_side=True, lower=True)
    backward = lax.linalg.triangular_solve(cholesky_low, forward, left_side=True, lower=True, transpose_a=True)
    return backward.T

def reference(tile_values, tile_coords, tile_count, owner_map, corner_factor, seg_factor):
    live_mask = (jnp.arange(TILES_DEV)[None, :] < tile_count[:, None]).reshape(-1)
    owner_slot = jnp.zeros((NBLK,), jnp.int32).at[owner_map].set(jnp.arange(NBLK, dtype=jnp.int32))
    corner_blocks = corner_factor.reshape(CORNERS // CBLK, CBLK, R)
    seg_blocks = seg_factor.reshape(SEGS // SEGB, SEGB, R)

    def add_tile(total, packed):
        values, coords, live = packed
        corner_rows = lax.dynamic_index_in_dim(corner_blocks, coords[0].astype(jnp.int32), 0, keepdims=False).astype(jnp.float32)
        seg_rows = lax.dynamic_index_in_dim(seg_blocks, coords[2].astype(jnp.int32), 0, keepdims=False).astype(jnp.float32)
        khatri = (corner_rows[:, None, :] * seg_rows[None, :, :]).astype(jnp.bfloat16)
        khatri = lax.optimization_barrier(khatri)
        khatri = khatri.reshape(CBLK * SEGB, R).astype(jnp.float32)
        term = jnp.dot(values.astype(jnp.float32), khatri, precision=lax.Precision.HIGHEST)
        term = jnp.where(live, term, jnp.zeros_like(term))
        start = (owner_slot[coords[1]] * NETB).astype(jnp.int32)
        former = lax.dynamic_slice_in_dim(total, start, NETB, 0)
        return (lax.dynamic_update_slice_in_dim(total, former + term, start, 0), None)
    mttkrp, _ = lax.scan(add_tile, jnp.zeros((NBLK * NETB, R), jnp.float32), (tile_values, tile_coords, live_mask))
    corner_gram = jnp.dot(corner_factor.T.astype(jnp.float32), corner_factor.astype(jnp.float32), preferred_element_type=jnp.float32)
    seg_gram = jnp.dot(seg_factor.T.astype(jnp.float32), seg_factor.astype(jnp.float32), preferred_element_type=jnp.float32)
    return solve_rows(corner_gram * seg_gram, mttkrp)
```

```python
import jax
import jax.numpy as jnp
from jax import lax
from jax.experimental import pallas as pl
from jax.experimental.pallas import tpu as pltpu
from jax.sharding import Mesh, PartitionSpec as P

CBLK = 8
ALL = ("net", "y", "core", "corner")
HIGH = lax.Precision.HIGHEST


def mm(a, b):
    return jnp.dot(a, b, precision=HIGH, preferred_element_type=jnp.float32)


def invert_block(a):
    n = a.shape[0]
    lane = lax.broadcasted_iota(jnp.int32, (1, n), 1)
    sub = lax.broadcasted_iota(jnp.int32, (n, 1), 0)
    for k in range(0, n, 2):
        r1 = a[k : k + 1, :]
        r2 = a[k + 1 : k + 2, :]
        c1 = a[:, k : k + 1]
        c2 = a[:, k + 1 : k + 2]
        p11 = r1[:, k : k + 1]
        p12 = r1[:, k + 1 : k + 2]
        p22 = r2[:, k + 1 : k + 2]
        inv = 1.0 / (p11 * p22 - p12 * p12)
        q11 = p22 * inv
        q12 = -p12 * inv
        q22 = p11 * inv
        in1 = lane == k
        in2 = lane == k + 1
        n1 = jnp.where(in1, q11, jnp.where(in2, q12, q11 * r1 + q12 * r2))
        n2 = jnp.where(in1, q12, jnp.where(in2, q22, q12 * r1 + q22 * r2))
        row1 = sub == k
        row2 = sub == k + 1
        m1 = jnp.where(row1, -1.0, jnp.where(row2, 0.0, c1))
        m2 = jnp.where(row2, -1.0, jnp.where(row1, 0.0, c2))
        kept = jnp.where(in1 | in2 | row1 | row2, 0.0, a)
        a = kept - m1 * n1 - m2 * n2
    return a


def inverse_kernel(gram_ref, corner_ref, out_ref):
    corner = corner_ref[...]
    gram = gram_ref[...] * lax.dot_general(
        corner, corner, (((0,), (0,)), ((), ())), preferred_element_type=jnp.float32
    )
    h = gram.shape[0] // 2
    a12 = gram[:h, h:]
    a21 = gram[h:, :h]
    p = invert_block(gram[:h, :h])
    w = mm(p, a12)
    v = mm(a21, p)
    q = invert_block(gram[h:, h:] - mm(a21, w))
    wq = mm(w, q)
    out_ref[:h, :h] = p + mm(wq, v)
    out_ref[:h, h:] = -wq
    out_ref[h:, :h] = -mm(q, v)
    out_ref[h:, h:] = q


def contract_kernel(
    seg_ids, corner_ids, side_ids, slot_ids, live_ids, values_ref, seg_ref, corner_ref, keep_ref, send_ref
):
    step = pl.program_id(0)

    @pl.when(step == 0)
    def _():
        keep_ref[...] = jnp.zeros_like(keep_ref)
        send_ref[...] = jnp.zeros_like(send_ref)

    seg_rows = seg_ref[0].astype(jnp.float32)
    corner_rows = corner_ref[corner_ids[step]].astype(jnp.float32)
    khatri = jnp.concatenate(
        [(corner_rows[a : a + 1, :] * seg_rows).astype(jnp.bfloat16) for a in range(CBLK)], axis=0
    )
    part = jnp.dot(values_ref[0], khatri, preferred_element_type=jnp.float32)
    slot = slot_ids[step]
    live = live_ids[step] == 1
    kept = side_ids[step] == 0

    @pl.when(live & kept)
    def _():
        keep_ref[slot] += part

    @pl.when(live & jnp.logical_not(kept))
    def _():
        send_ref[slot] += part


def whiten_kernel(keep_ref, recv_ref, inv_ref, out_ref):
    rows = keep_ref[0] + recv_ref[0]
    out_ref[0] = mm(rows, inv_ref[...]).astype(jnp.bfloat16)


def body(tile_values, tile_coords, tile_count, owner_map, corner_factor, seg_factor):
    tiles, net_rows, width = tile_values.shape
    cols = corner_factor.shape[1]
    seg_width = width // CBLK
    nz = lax.axis_size("net")
    ny = lax.axis_size("y")
    nx = lax.axis_size("corner")
    core = lax.axis_index("core")
    xi = lax.axis_index("corner")
    seg_i = lax.axis_index("y") * lax.axis_size("core") + core
    per_corner = corner_factor.shape[0] // CBLK
    held = seg_factor.shape[0] // seg_width
    owners = ny * nx

    gathered = lax.all_gather(seg_factor, "net", axis=0, tiled=True)

    seg_part = lax.dot_general(
        seg_factor, seg_factor, (((0,), (0,)), ((), ())), preferred_element_type=jnp.float32
    )
    share = cols // nx
    mine = lax.dynamic_slice_in_dim(seg_part, xi * share, share, 0)
    halves = cols // 128
    chunks = mine.reshape(share // 8, 8, halves, 128).transpose(0, 2, 1, 3).reshape(nz, -1, 128)
    chunk = jnp.sum(lax.all_to_all(chunks, "net", 0, 0), axis=0)
    spread = jnp.broadcast_to(chunk[None], (ny * lax.axis_size("core"),) + chunk.shape)
    chunk = jnp.sum(lax.all_to_all(spread, ("y", "core"), 0, 0), axis=0)
    crows = corner_factor.shape[0] // nz
    zi = lax.axis_index("net")
    own = lax.dynamic_slice_in_dim(corner_factor, zi * crows, crows, 0)
    own = own.astype(jnp.float32).reshape(crows * halves, 128)
    own = jnp.pad(own, ((0, 8 - crows * halves), (0, 0)))
    packet = jnp.concatenate([chunk, own], axis=0)
    packet = jnp.broadcast_to(packet[None], (nz * nx,) + packet.shape)
    packet = lax.all_to_all(packet, ("net", "corner"), 0, 0)
    rows8 = chunk.shape[0]
    seg_gram = packet[:, :rows8].reshape(share // 8, halves, nx, 8, 128)
    seg_gram = seg_gram.transpose(2, 0, 3, 1, 4).reshape(cols, cols)
    corner_all = packet[:, rows8 : rows8 + crows * halves].reshape(-1, cols).astype(jnp.bfloat16)
    inverse = pl.pallas_call(
        inverse_kernel,
        out_shape=jax.ShapeDtypeStruct((cols, cols), jnp.float32),
        compiler_params=pltpu.CompilerParams(vmem_limit_bytes=32 << 20),
        name="gram_inverse",
    )(seg_gram, corner_all)

    corner_ids = jnp.clip(tile_coords[:, 0] - xi * per_corner, 0, per_corner - 1)
    seg_ids = jnp.clip(tile_coords[:, 2] - seg_i * (held * nz), 0, held * nz - 1)
    match = tile_coords[:, 1][:, None] == owner_map[None, :]
    slot = jnp.sum(jnp.where(match, jnp.arange(owner_map.shape[0], dtype=jnp.int32)[None, :], 0), axis=1)
    side_ids = ((slot // nx) % 2 != core).astype(jnp.int32)
    slot_ids = (slot // (2 * nx)) * nx + slot % nx
    live_ids = (jnp.arange(tiles, dtype=jnp.int32) < tile_count[0]).astype(jnp.int32)

    keep, send = pl.pallas_call(
        contract_kernel,
        grid_spec=pltpu.PrefetchScalarGridSpec(
            num_scalar_prefetch=5,
            grid=(tiles,),
            in_specs=[
                pl.BlockSpec((1, net_rows, width), lambda t, *_: (t, 0, 0)),
                pl.BlockSpec((1, seg_width, cols), lambda t, seg_ids, *_: (seg_ids[t], 0, 0)),
                pl.BlockSpec((per_corner, CBLK, cols), lambda t, *_: (0, 0, 0)),
            ],
            out_specs=[
                pl.BlockSpec((owners, net_rows, cols), lambda t, *_: (0, 0, 0)),
                pl.BlockSpec((owners, net_rows, cols), lambda t, *_: (0, 0, 0)),
            ],
        ),
        out_shape=[jax.ShapeDtypeStruct((owners, net_rows, cols), jnp.float32)] * 2,
        compiler_params=pltpu.CompilerParams(vmem_limit_bytes=48 << 20),
        name="contract",
    )(
        seg_ids,
        corner_ids,
        side_ids,
        slot_ids,
        live_ids,
        tile_values,
        gathered.reshape(-1, seg_width, cols),
        corner_factor.reshape(per_corner, CBLK, cols),
    )
    received = lax.ppermute(send, "core", [(0, 1), (1, 0)])
    block = pl.BlockSpec((1, net_rows, cols), lambda t: (t, 0, 0))
    solved = pl.pallas_call(
        whiten_kernel,
        grid=(owners,),
        in_specs=[block, block, pl.BlockSpec((cols, cols), lambda t: (0, 0))],
        out_specs=block,
        out_shape=jax.ShapeDtypeStruct((owners, net_rows, cols), jnp.bfloat16),
        name="apply_inverse",
    )(keep, received, inverse)
    shares = lax.all_to_all(solved, ("y", "corner"), 0, 0)
    return jnp.sum(shares.astype(jnp.float32), axis=0)


def solution(mesh):
    nz, seg, nx = mesh.devices.shape
    split = Mesh(mesh.devices.reshape(nz, seg // 2, 2, nx), ALL)
    return jax.shard_map(
        body,
        mesh=split,
        in_specs=(
            P(ALL, None, None),
            P(ALL, None),
            P(ALL),
            P("net"),
            P("corner", None),
            P(("y", "core", "net"), None),
        ),
        out_specs=P(ALL, None),
        check_vma=False,
    )
```

```python
import jax
import jax.numpy as jnp
from jax import lax
from jax.experimental import pallas as pl
from jax.experimental.pallas import tpu as pltpu
from jax.sharding import Mesh, PartitionSpec as P

CBLK = 8
GRP = 4
PIVOTS = 4
ALL = ("net", "y", "core", "corner")
HIGH = lax.Precision.HIGHEST


def mm(a, b):
    return jnp.dot(a, b, precision=HIGH, preferred_element_type=jnp.float32)


def invert_pivot(p):
    m = len(p)
    if m == 2:
        inv = 1.0 / (p[0][0] * p[1][1] - p[0][1] * p[0][1])
        off = -p[0][1] * inv
        return [[p[1][1] * inv, off], [off, p[0][0] * inv]]
    h = m // 2
    r = range(h)
    ai = invert_pivot([row[:h] for row in p[:h]])
    b = [row[h:] for row in p[:h]]
    w = [[sum(ai[i][l] * b[l][j] for l in r) for j in r] for i in r]
    s = [[p[h + i][h + j] - sum(b[l][min(i, j)] * w[l][max(i, j)] for l in r) for j in r] for i in r]
    q = invert_pivot(s)
    wq = [[sum(w[i][l] * q[l][j] for l in r) for j in r] for i in r]
    top = [[ai[i][j] + sum(wq[i][l] * w[j][l] for l in r) for j in r] for i in r]
    return [top[i] + [-x for x in wq[i]] for i in r] + [[-wq[j][i] for j in r] + q[i] for i in r]


def invert_block(a):
    n = a.shape[0]
    m = PIVOTS
    lane = lax.broadcasted_iota(jnp.int32, (1, n), 1)
    sub = lax.broadcasted_iota(jnp.int32, (n, 1), 0)
    for k in range(0, n, m):
        rows = [a[k + i : k + i + 1, :] for i in range(m)]
        p = [[None] * m for _ in range(m)]
        for i in range(m):
            for j in range(i, m):
                p[i][j] = p[j][i] = jnp.broadcast_to(rows[i][:, k + j : k + j + 1], (1, n))
        q = invert_pivot(p)
        in_lane = (lane >= k) & (lane < k + m)
        in_sub = (sub >= k) & (sub < k + m)
        new = jnp.where(in_lane | in_sub, 0.0, a)
        for i in range(m):
            row = sum(q[i][j] * rows[j] for j in range(m))
            for j in range(m):
                row = jnp.where(lane == k + j, q[i][j], row)
            col = jnp.where(in_sub, jnp.where(sub == k + i, -1.0, 0.0), a[:, k + i : k + i + 1])
            new = new - col * row
        a = new
    return a


def inverse_kernel(packet_ref, out_ref):
    cols = out_ref.shape[1]
    packet = packet_ref[...]
    corner = packet[:, 8:, :].reshape(-1, cols).astype(jnp.bfloat16)
    gram = packet[:, :8, :].reshape(-1, cols) * lax.dot_general(
        corner, corner, (((0,), (0,)), ((), ())), preferred_element_type=jnp.float32
    )
    h = cols // 2
    a12 = gram[:h, h:]
    a21 = gram[h:, :h]
    p = invert_block(gram[:h, :h])
    w = mm(p, a12)
    v = mm(a21, p)
    q = invert_block(gram[h:, h:] - mm(a21, w))
    wq = mm(w, q)
    out_ref[:h, :h] = p + mm(wq, v)
    out_ref[:h, h:] = -wq
    out_ref[h:, :h] = -mm(q, v)
    out_ref[h:, h:] = q


def contract_kernel(seg_ids, corner_ids, side_ids, slot_ids, live_ids, values_ref, *refs):
    seg_refs, (corner_ref, keep_ref, send_ref) = refs[:GRP], refs[GRP:]
    step = pl.program_id(0)

    @pl.when(step == 0)
    def _():
        keep_ref[...] = jnp.zeros_like(keep_ref)
        send_ref[...] = jnp.zeros_like(send_ref)

    for g in range(GRP):
        t = step * GRP + g
        seg_rows = seg_refs[g][0].astype(jnp.float32)
        corner_rows = corner_ref[corner_ids[t]].astype(jnp.float32)
        khatri = jnp.concatenate(
            [(corner_rows[a : a + 1, :] * seg_rows).astype(jnp.bfloat16) for a in range(CBLK)], axis=0
        )
        part = jnp.dot(values_ref[g], khatri, preferred_element_type=jnp.float32)
        slot = slot_ids[t]
        live = live_ids[t] == 1
        kept = side_ids[t] == 0

        @pl.when(live & kept)
        def _(part=part, slot=slot):
            keep_ref[slot] += part

        @pl.when(live & jnp.logical_not(kept))
        def _(part=part, slot=slot):
            send_ref[slot] += part


def split(x):
    high = x.astype(jnp.bfloat16)
    return high, (x - high.astype(jnp.float32)).astype(jnp.bfloat16)


def whiten_kernel(keep_ref, recv_ref, inv_ref, out_ref):
    inv_high, inv_low = split(inv_ref[...])

    def block(i, carry):
        rows_high, rows_low = split(keep_ref[i] + recv_ref[i])
        out = jnp.dot(rows_high, inv_low, preferred_element_type=jnp.float32)
        out += jnp.dot(rows_low, inv_high, preferred_element_type=jnp.float32)
        out += jnp.dot(rows_high, inv_high, preferred_element_type=jnp.float32)
        out_ref[i] = out.astype(jnp.bfloat16)
        return carry

    lax.fori_loop(0, keep_ref.shape[0], block, 0, unroll=4)


def body(tile_values, tile_coords, tile_count, owner_map, corner_factor, seg_factor):
    tiles, net_rows, width = tile_values.shape
    cols = corner_factor.shape[1]
    seg_width = width // CBLK
    nz = lax.axis_size("net")
    ny = lax.axis_size("y")
    nx = lax.axis_size("corner")
    core = lax.axis_index("core")
    xi = lax.axis_index("corner")
    seg_i = lax.axis_index("y") * lax.axis_size("core") + core
    per_corner = corner_factor.shape[0] // CBLK
    held = seg_factor.shape[0] // seg_width
    owners = ny * nx

    gathered = lax.all_gather(seg_factor, "net", axis=0, tiled=True)

    seg_part = lax.dot_general(
        seg_factor, seg_factor, (((0,), (0,)), ((), ())), preferred_element_type=jnp.float32
    )
    nseg = ny * lax.axis_size("core")
    mine = lax.dynamic_index_in_dim(seg_part.reshape(nseg, nx, -1, cols), xi, 1, keepdims=False)
    chunk = jnp.sum(lax.all_to_all(mine, ("y", "core"), 0, 0), axis=0)
    chunk = jnp.sum(lax.all_to_all(jnp.broadcast_to(chunk[None], (nz,) + chunk.shape), "net", 0, 0), axis=0)
    crows = corner_factor.shape[0] // nseg
    own = lax.dynamic_slice_in_dim(corner_factor, seg_i * crows, crows, 0).astype(jnp.float32)
    packet = jnp.concatenate([chunk, jnp.pad(own, ((0, 8 - crows), (0, 0)))], axis=0)
    packet = jnp.broadcast_to(packet[None], (nseg * nx,) + packet.shape)
    packet = lax.all_to_all(packet, ("y", "core", "corner"), 0, 0)
    inverse = pl.pallas_call(
        inverse_kernel,
        out_shape=jax.ShapeDtypeStruct((cols, cols), jnp.float32),
        compiler_params=pltpu.CompilerParams(vmem_limit_bytes=32 << 20),
        name="gram_inverse",
    )(packet)
    gathered, inverse = lax.optimization_barrier((gathered, inverse))

    corner_ids = jnp.clip(tile_coords[:, 0] - xi * per_corner, 0, per_corner - 1)
    seg_ids = jnp.clip(tile_coords[:, 2] - seg_i * (held * nz), 0, held * nz - 1)
    match = tile_coords[:, 1][:, None] == owner_map[None, :]
    slot = jnp.sum(jnp.where(match, jnp.arange(owner_map.shape[0], dtype=jnp.int32)[None, :], 0), axis=1)
    side_ids = ((slot // nx) % 2 != core).astype(jnp.int32)
    slot_ids = (slot // (2 * nx)) * nx + slot % nx
    live_ids = (jnp.arange(tiles, dtype=jnp.int32) < tile_count[0]).astype(jnp.int32)

    blocks = gathered.reshape(-1, seg_width, cols)

    def seg_spec(g):
        return pl.BlockSpec((1, seg_width, cols), lambda t, ids, *_: (ids[t * GRP + g], 0, 0))

    keep, send = pl.pallas_call(
        contract_kernel,
        grid_spec=pltpu.PrefetchScalarGridSpec(
            num_scalar_prefetch=5,
            grid=(tiles // GRP,),
            in_specs=[
                pl.BlockSpec((GRP, net_rows, width), lambda t, *_: (t, 0, 0)),
                *[seg_spec(g) for g in range(GRP)],
                pl.BlockSpec((per_corner, CBLK, cols), lambda t, *_: (0, 0, 0)),
            ],
            out_specs=[
                pl.BlockSpec((owners, net_rows, cols), lambda t, *_: (0, 0, 0)),
                pl.BlockSpec((owners, net_rows, cols), lambda t, *_: (0, 0, 0)),
            ],
        ),
        out_shape=[jax.ShapeDtypeStruct((owners, net_rows, cols), jnp.float32)] * 2,
        compiler_params=pltpu.CompilerParams(vmem_limit_bytes=48 << 20),
        name="contract",
    )(
        seg_ids,
        corner_ids,
        side_ids,
        slot_ids,
        live_ids,
        tile_values,
        *[blocks] * GRP,
        corner_factor.reshape(per_corner, CBLK, cols),
    )
    received = lax.ppermute(send, "core", [(0, 1), (1, 0)])
    solved = pl.pallas_call(
        whiten_kernel,
        out_shape=jax.ShapeDtypeStruct((owners, net_rows, cols), jnp.bfloat16),
        compiler_params=pltpu.CompilerParams(vmem_limit_bytes=32 << 20),
        name="apply_inverse",
    )(keep, received, inverse)
    shares = lax.all_to_all(solved, ("y", "corner"), 0, 0)
    return jnp.sum(shares.astype(jnp.float32), axis=0)


def solution(mesh):
    nz, seg, nx = mesh.devices.shape
    split = Mesh(mesh.devices.reshape(nz, seg // 2, 2, nx), ALL)
    return jax.shard_map(
        body,
        mesh=split,
        in_specs=(
            P(ALL, None, None),
            P(ALL, None),
            P(ALL),
            P("net"),
            P("corner", None),
            P(("y", "core", "net"), None),
        ),
        out_specs=P(ALL, None),
        check_vma=False,
    )
```

```python
import functools

import jax
import jax.numpy as jnp
from jax import lax
from jax.experimental import pallas as pl
from jax.experimental.pallas import tpu as pltpu
from jax.sharding import Mesh, PartitionSpec as P

CBLK = 8
GRP = 4
CAP = 2
PIVOTS = 4
NET = ("zh", "zl")
SEG = ("y", "core")
ALL = NET + SEG + ("corner",)
FREE = pl.CostEstimate(flops=0, transcendentals=0, bytes_accessed=0)
HIGH = lax.Precision.HIGHEST


def mm(a, b):
    return jnp.dot(a, b, precision=HIGH, preferred_element_type=jnp.float32)


def invert_pivot(p):
    m = len(p)
    if m == 2:
        inv = 1.0 / (p[0][0] * p[1][1] - p[0][1] * p[0][1])
        off = -p[0][1] * inv
        return [[p[1][1] * inv, off], [off, p[0][0] * inv]]
    h = m // 2
    r = range(h)
    ai = invert_pivot([row[:h] for row in p[:h]])
    b = [row[h:] for row in p[:h]]
    w = [[sum(ai[i][l] * b[l][j] for l in r) for j in r] for i in r]
    s = [[p[h + i][h + j] - sum(b[l][min(i, j)] * w[l][max(i, j)] for l in r) for j in r] for i in r]
    q = invert_pivot(s)
    wq = [[sum(w[i][l] * q[l][j] for l in r) for j in r] for i in r]
    top = [[ai[i][j] + sum(wq[i][l] * w[j][l] for l in r) for j in r] for i in r]
    return [top[i] + [-x for x in wq[i]] for i in r] + [[-wq[j][i] for j in r] + q[i] for i in r]


def invert_block(a):
    n = a.shape[0]
    m = PIVOTS
    lane = lax.broadcasted_iota(jnp.int32, (1, n), 1)
    sub = lax.broadcasted_iota(jnp.int32, (n, 1), 0)
    for k in range(0, n, m):
        rows = [a[k + i : k + i + 1, :] for i in range(m)]
        p = [[None] * m for _ in range(m)]
        for i in range(m):
            for j in range(i, m):
                p[i][j] = p[j][i] = jnp.broadcast_to(rows[i][:, k + j : k + j + 1], (1, n))
        q = invert_pivot(p)
        in_lane = (lane >= k) & (lane < k + m)
        in_sub = (sub >= k) & (sub < k + m)
        new = jnp.where(in_lane | in_sub, 0.0, a)
        for i in range(m):
            row = sum(q[i][j] * rows[j] for j in range(m))
            for j in range(m):
                row = jnp.where(lane == k + j, q[i][j], row)
            col = jnp.where(in_sub, jnp.where(sub == k + i, -1.0, 0.0), a[:, k + i : k + i + 1])
            new = new - col * row
        a = new
    return a


def inverse_kernel(packet_ref, out_ref):
    cols = out_ref.shape[1]
    packet = packet_ref[...]
    corner = packet[:, 8:, :].reshape(-1, cols).astype(jnp.bfloat16)
    gram = packet[:, :8, :].reshape(-1, cols) * lax.dot_general(
        corner, corner, (((0,), (0,)), ((), ())), preferred_element_type=jnp.float32
    )
    h = cols // 2
    a12 = gram[:h, h:]
    a21 = gram[h:, :h]
    p = invert_block(gram[:h, :h])
    w = mm(p, a12)
    v = mm(a21, p)
    q = invert_block(gram[h:, h:] - mm(a21, w))
    wq = mm(w, q)
    out_ref[:h, :h] = p + mm(wq, v)
    out_ref[:h, h:] = -wq
    out_ref[h:, :h] = -mm(q, v)
    out_ref[h:, h:] = q


def contract_kernel(seg_ids, corner_ids, side_ids, slot_ids, live_ids, values_ref, *refs):
    seg_refs, (corner_ref, keep_ref, send_ref) = refs[:-3], refs[-3:]
    per = seg_refs[0].shape[0]
    step = pl.program_id(0)

    @pl.when(step == 0)
    def _():
        keep_ref[...] = jnp.zeros_like(keep_ref)
        send_ref[...] = jnp.zeros_like(send_ref)

    for g in range(GRP):
        t = step * GRP + g
        place = seg_ids[t]
        seg_rows = lax.switch(
            place // per, [lambda at, ref=ref: ref[at] for ref in seg_refs], place % per
        ).astype(jnp.float32)
        corner_rows = corner_ref[corner_ids[t]].astype(jnp.float32)
        khatri = jnp.concatenate(
            [(corner_rows[a : a + 1, :] * seg_rows).astype(jnp.bfloat16) for a in range(CBLK)], axis=0
        )
        part = jnp.dot(values_ref[g], khatri, preferred_element_type=jnp.float32)
        slot = slot_ids[t]
        live = live_ids[t] == 1
        kept = side_ids[t] == 0

        @pl.when(live & kept)
        def _(part=part, slot=slot):
            keep_ref[slot] += part

        @pl.when(live & jnp.logical_not(kept))
        def _(part=part, slot=slot):
            send_ref[slot] += part


def request_kernel(coords_ref, slot_ref, request_ref, *, held, holders, near):
    seg_i = lax.axis_index("y") * lax.axis_size("core") + lax.axis_index("core")
    request_ref[...] = jnp.zeros_like(request_ref)
    seen = []
    for t in range(coords_ref.shape[0]):
        local = jnp.clip(coords_ref[t, 2] - seg_i * (held * holders), 0, held * holders - 1)
        holder = local // held
        rank = jnp.int32(0)
        for other in seen:
            rank += (other == holder).astype(jnp.int32)
        rank = jnp.minimum(rank, CAP - 1)
        seen.append(holder)
        shift = lax.rem(lax.axis_index("corner") - holder // near + near, near)
        slot_ref[t] = shift * (near * CAP) + (holder % near) * CAP + rank
        row = jnp.full((1, request_ref.shape[2]), local % held, jnp.int32)
        request_ref[holder // near, pl.ds((holder % near) * CAP + rank, 1), :] = row


def select_kernel(req_ref, *refs):
    hold = len(refs) // 2
    parts, outs = refs[:hold], refs[hold:]
    zl = lax.axis_index("zl")
    xi = lax.axis_index("corner")
    for offset in range(hold):
        residue = lax.rem(zl + offset, hold)
        for shift in range(hold):
            dest = lax.rem(xi + shift, hold)
            for rank in range(CAP):
                slot = residue * CAP + rank
                outs[shift][slot] = parts[offset][req_ref[dest, slot]]


def split(x):
    high = x.astype(jnp.bfloat16)
    return high, (x - high.astype(jnp.float32)).astype(jnp.bfloat16)


def whiten_kernel(keep_ref, recv_ref, inv_ref, out_ref):
    inv_high, inv_low = split(inv_ref[...])

    def block(i, carry):
        rows_high, rows_low = split(keep_ref[i] + recv_ref[i])
        out = jnp.dot(rows_high, inv_low, preferred_element_type=jnp.float32)
        out += jnp.dot(rows_low, inv_high, preferred_element_type=jnp.float32)
        out += jnp.dot(rows_high, inv_high, preferred_element_type=jnp.float32)
        out_ref[i] = out.astype(jnp.bfloat16)
        return carry

    lax.fori_loop(0, keep_ref.shape[0], block, 0, unroll=4)


def body(tile_values, tile_coords, tile_count, owner_map, corner_factor, seg_factor):
    tiles, net_rows, width = tile_values.shape
    cols = corner_factor.shape[1]
    seg_width = width // CBLK
    nz = lax.axis_size(NET)
    ny = lax.axis_size("y")
    nx = lax.axis_size("corner")
    core = lax.axis_index("core")
    xi = lax.axis_index("corner")
    seg_i = lax.axis_index("y") * lax.axis_size("core") + core
    per_corner = corner_factor.shape[0] // CBLK
    held = seg_factor.shape[0] // seg_width
    owners = ny * nx

    near = nz // nx
    far = [
        (h * nx + x, (h + near * ((x + h) % nx)) % nz * nx + h // near)
        for h in range(nz)
        for x in range(nx)
    ]
    own_rows = lax.ppermute(seg_factor, NET + ("corner",), far)
    slot_of, request = pl.pallas_call(
        functools.partial(request_kernel, held=held, holders=nz, near=near),
        in_specs=[pl.BlockSpec(memory_space=pltpu.SMEM)],
        out_specs=[pl.BlockSpec(memory_space=pltpu.SMEM), pl.BlockSpec(memory_space=pltpu.VMEM)],
        out_shape=[
            jax.ShapeDtypeStruct((tiles,), jnp.int32),
            jax.ShapeDtypeStruct((nx, near * CAP, 128), jnp.int32),
        ],
        cost_estimate=FREE,
        name="requests",
    )(tile_coords)
    request = lax.all_to_all(request, "corner", 0, 0)[:, :, 0]
    request = jnp.clip(request, 0, held - 1)
    own_rows, request = lax.optimization_barrier((own_rows, request))
    up = lax.ppermute(own_rows, NET, [((z + 1) % nz, z) for z in range(nz)])
    two = lax.ppermute(own_rows, NET, [((z + (2 if z % 2 else -2)) % nz, z) for z in range(nz)])
    down = lax.ppermute(own_rows, NET, [((z - 1) % nz, z) for z in range(nz)])
    nseg = lax.axis_size(SEG)
    seg_part = lax.dot_general(
        own_rows, own_rows, (((0,), (0,)), ((), ())), preferred_element_type=jnp.float32
    )
    shares = lax.all_to_all(seg_part.reshape(nseg * nx, -1, cols), SEG + ("corner",), 0, 0)
    chunk = jnp.sum(shares, axis=0)
    up, two, down, chunk = lax.optimization_barrier((up, two, down, chunk))
    smem = pl.BlockSpec(memory_space=pltpu.SMEM)
    vmem = pl.BlockSpec(memory_space=pltpu.VMEM)
    chosen = pl.pallas_call(
        select_kernel,
        in_specs=[smem] + [vmem] * near,
        out_specs=[vmem] * nx,
        out_shape=[jax.ShapeDtypeStruct((near * CAP, seg_width, cols), seg_factor.dtype)] * nx,
        compiler_params=pltpu.CompilerParams(vmem_limit_bytes=32 << 20),
        cost_estimate=FREE,
        name="select_blocks",
    )(request, *(v.reshape(held, seg_width, cols) for v in (own_rows, up, two, down)))
    chunk = jnp.sum(lax.all_to_all(jnp.broadcast_to(chunk[None], (near,) + chunk.shape), "zl", 0, 0), axis=0)
    crows = corner_factor.shape[0] // nseg
    own = lax.dynamic_slice_in_dim(corner_factor, seg_i * crows, crows, 0).astype(jnp.float32)
    packet = jnp.concatenate([chunk, jnp.pad(own, ((0, 8 - crows), (0, 0)))], axis=0)
    packet = jnp.broadcast_to(packet[None], (nseg * nx,) + packet.shape)
    packet = lax.all_to_all(packet, SEG + ("corner",), 0, 0)
    blocks = [chosen[0]] + [
        lax.ppermute(chosen[k], "corner", [(x, (x + k) % nx) for x in range(nx)]) for k in range(1, nx)
    ]
    inverse = pl.pallas_call(
        inverse_kernel,
        out_shape=jax.ShapeDtypeStruct((cols, cols), jnp.float32),
        compiler_params=pltpu.CompilerParams(vmem_limit_bytes=32 << 20),
        cost_estimate=FREE,
        name="gram_inverse",
    )(packet)

    blocks, inverse = lax.optimization_barrier((blocks, inverse))
    corner_ids = jnp.clip(tile_coords[:, 0] - xi * per_corner, 0, per_corner - 1)
    match = tile_coords[:, 1][:, None] == owner_map[None, :]
    slot = jnp.sum(jnp.where(match, jnp.arange(owner_map.shape[0], dtype=jnp.int32)[None, :], 0), axis=1)
    side_ids = ((slot // nx) % 2 != core).astype(jnp.int32)
    slot_ids = (slot // (2 * nx)) * nx + slot % nx
    live_ids = (jnp.arange(tiles, dtype=jnp.int32) < tile_count[0]).astype(jnp.int32)

    keep, send = pl.pallas_call(
        contract_kernel,
        grid_spec=pltpu.PrefetchScalarGridSpec(
            num_scalar_prefetch=5,
            grid=(tiles // GRP,),
            in_specs=[
                pl.BlockSpec((GRP, net_rows, width), lambda t, *_: (t, 0, 0)),
                *[vmem] * nx,
                pl.BlockSpec((per_corner, CBLK, cols), lambda t, *_: (0, 0, 0)),
            ],
            out_specs=[
                pl.BlockSpec((owners, net_rows, cols), lambda t, *_: (0, 0, 0)),
                pl.BlockSpec((owners, net_rows, cols), lambda t, *_: (0, 0, 0)),
            ],
        ),
        out_shape=[jax.ShapeDtypeStruct((owners, net_rows, cols), jnp.float32)] * 2,
        compiler_params=pltpu.CompilerParams(vmem_limit_bytes=48 << 20),
        name="contract",
    )(
        slot_of,
        corner_ids,
        side_ids,
        slot_ids,
        live_ids,
        tile_values,
        *blocks,
        corner_factor.reshape(per_corner, CBLK, cols),
    )
    received = lax.ppermute(send, "core", [(0, 1), (1, 0)])
    solved = pl.pallas_call(
        whiten_kernel,
        out_shape=jax.ShapeDtypeStruct((owners, net_rows, cols), jnp.bfloat16),
        compiler_params=pltpu.CompilerParams(vmem_limit_bytes=32 << 20),
        name="apply_inverse",
    )(keep, received, inverse)
    shares = lax.all_to_all(solved, ("y", "corner"), 0, 0)
    return jnp.sum(shares.astype(jnp.float32), axis=0)


def solution(mesh):
    nz, seg, nx = mesh.devices.shape
    split = Mesh(mesh.devices.reshape(nz // nx, nx, seg // 2, 2, nx), ALL)
    return jax.shard_map(
        body,
        mesh=split,
        in_specs=(
            P(ALL, None, None),
            P(ALL, None),
            P(ALL),
            P(NET),
            P("corner", None),
            P(SEG + NET, None),
        ),
        out_specs=P(ALL, None),
        check_vma=False,
    )
```

```python
import jax
import jax.numpy as jnp
from jax import lax
from jax.experimental import pallas as pl
from jax.experimental.pallas import tpu as pltpu
from jax.sharding import Mesh, PartitionSpec as P

CBLK = 8
GRP = 8
PIVOTS = 4
NET = ("zh", "zl")
SEG = ("y", "core")
ALL = NET + SEG + ("corner",)
HIGH = lax.Precision.HIGHEST


def mm(a, b):
    return jnp.dot(a, b, precision=HIGH, preferred_element_type=jnp.float32)


def invert_pivot(p):
    m = len(p)
    if m == 2:
        inv = 1.0 / (p[0][0] * p[1][1] - p[0][1] * p[0][1])
        off = -p[0][1] * inv
        return [[p[1][1] * inv, off], [off, p[0][0] * inv]]
    h = m // 2
    r = range(h)
    ai = invert_pivot([row[:h] for row in p[:h]])
    b = [row[h:] for row in p[:h]]
    w = [[sum(ai[i][l] * b[l][j] for l in r) for j in r] for i in r]
    s = [[p[h + i][h + j] - sum(b[l][min(i, j)] * w[l][max(i, j)] for l in r) for j in r] for i in r]
    q = invert_pivot(s)
    wq = [[sum(w[i][l] * q[l][j] for l in r) for j in r] for i in r]
    top = [[ai[i][j] + sum(wq[i][l] * w[j][l] for l in r) for j in r] for i in r]
    return [top[i] + [-x for x in wq[i]] for i in r] + [[-wq[j][i] for j in r] + q[i] for i in r]


def invert_block(a):
    n = a.shape[0]
    m = PIVOTS
    lane = lax.broadcasted_iota(jnp.int32, (1, n), 1)
    sub = lax.broadcasted_iota(jnp.int32, (n, 1), 0)
    for k in range(0, n, m):
        rows = [a[k + i : k + i + 1, :] for i in range(m)]
        p = [[None] * m for _ in range(m)]
        for i in range(m):
            for j in range(i, m):
                p[i][j] = p[j][i] = jnp.broadcast_to(rows[i][:, k + j : k + j + 1], (1, n))
        q = invert_pivot(p)
        in_lane = (lane >= k) & (lane < k + m)
        in_sub = (sub >= k) & (sub < k + m)
        new = jnp.where(in_lane | in_sub, 0.0, a)
        for i in range(m):
            row = sum(q[i][j] * rows[j] for j in range(m))
            for j in range(m):
                row = jnp.where(lane == k + j, q[i][j], row)
            col = jnp.where(in_sub, jnp.where(sub == k + i, -1.0, 0.0), a[:, k + i : k + i + 1])
            new = new - col * row
        a = new
    return a


def inverse_kernel(packet_ref, out_ref):
    cols = out_ref.shape[1]
    packet = packet_ref[...]
    corner = packet[:, 8:, :].reshape(-1, cols).astype(jnp.bfloat16)
    gram = packet[:, :8, :].reshape(-1, cols) * lax.dot_general(
        corner, corner, (((0,), (0,)), ((), ())), preferred_element_type=jnp.float32
    )
    h = cols // 2
    a12 = gram[:h, h:]
    a21 = gram[h:, :h]
    p = invert_block(gram[:h, :h])
    w = mm(p, a12)
    v = mm(a21, p)
    q = invert_block(gram[h:, h:] - mm(a21, w))
    wq = mm(w, q)
    out_ref[:h, :h] = p + mm(wq, v)
    out_ref[:h, h:] = -wq
    out_ref[h:, :h] = -mm(q, v)
    out_ref[h:, h:] = q


def contract_kernel(seg_ids, corner_ids, keep_ids, send_ids, values_ref, *refs):
    seg_refs, (corner_ref, keep_ref, send_ref) = refs[:GRP], refs[GRP:]
    step = pl.program_id(0)

    @pl.when(step == 0)
    def _():
        keep_ref[...] = jnp.zeros_like(keep_ref)
        send_ref[...] = jnp.zeros_like(send_ref)

    for g in range(GRP):
        t = step * GRP + g
        seg_rows = seg_refs[g][0].astype(jnp.float32)
        corner_rows = corner_ref[corner_ids[t]].astype(jnp.float32)
        khatri = jnp.concatenate(
            [(corner_rows[a : a + 1, :] * seg_rows).astype(jnp.bfloat16) for a in range(CBLK)], axis=0
        )
        part = jnp.dot(values_ref[g], khatri, preferred_element_type=jnp.float32)
        keep_ref[keep_ids[t]] += part
        send_ref[send_ids[t]] += part


def split(x):
    high = x.astype(jnp.bfloat16)
    return high, (x - high.astype(jnp.float32)).astype(jnp.bfloat16)


def whiten_kernel(keep_ref, recv_ref, inv_ref, out_ref):
    inv_high, inv_low = split(inv_ref[...])

    def block(i, carry):
        rows_high, rows_low = split(keep_ref[i] + recv_ref[i])
        out = jnp.dot(rows_high, inv_low, preferred_element_type=jnp.float32)
        out += jnp.dot(rows_low, inv_high, preferred_element_type=jnp.float32)
        out += jnp.dot(rows_high, inv_high, preferred_element_type=jnp.float32)
        out_ref[i] = out.astype(jnp.bfloat16)
        return carry

    lax.fori_loop(0, out_ref.shape[0], block, 0, unroll=4)


def body(tile_values, tile_coords, tile_count, owner_map, corner_factor, seg_factor):
    tiles, net_rows, width = tile_values.shape
    cols = corner_factor.shape[1]
    seg_width = width // CBLK
    nz = lax.axis_size(NET)
    ny = lax.axis_size("y")
    nx = lax.axis_size("corner")
    core = lax.axis_index("core")
    xi = lax.axis_index("corner")
    seg_i = lax.axis_index("y") * lax.axis_size("core") + core
    per_corner = corner_factor.shape[0] // CBLK
    held = seg_factor.shape[0] // seg_width
    owners = ny * nx

    gathered = lax.all_gather(seg_factor, NET, axis=0, tiled=True)

    seg_part = lax.dot_general(
        seg_factor, seg_factor, (((0,), (0,)), ((), ())), preferred_element_type=jnp.float32
    )
    nseg = ny * lax.axis_size("core")
    mine = lax.dynamic_index_in_dim(seg_part.reshape(nseg, nx, -1, cols), xi, 1, keepdims=False)
    chunk = jnp.sum(lax.all_to_all(mine, SEG, 0, 0), axis=0)
    for axis in NET:
        spread = jnp.broadcast_to(chunk[None], (lax.axis_size(axis),) + chunk.shape)
        chunk = jnp.sum(lax.all_to_all(spread, axis, 0, 0), axis=0)
    crows = corner_factor.shape[0] // nseg
    own = lax.dynamic_slice_in_dim(corner_factor, seg_i * crows, crows, 0).astype(jnp.float32)
    packet = jnp.concatenate([chunk, jnp.pad(own, ((0, 8 - crows), (0, 0)))], axis=0)
    packet = jnp.broadcast_to(packet[None], (nseg * nx,) + packet.shape)
    packet = lax.all_to_all(packet, SEG + ("corner",), 0, 0)
    inverse = pl.pallas_call(
        inverse_kernel,
        out_shape=jax.ShapeDtypeStruct((cols, cols), jnp.float32),
        compiler_params=pltpu.CompilerParams(vmem_limit_bytes=32 << 20),
        name="gram_inverse",
    )(packet)
    gathered, inverse = lax.optimization_barrier((gathered, inverse))

    corner_ids = jnp.clip(tile_coords[:, 0] - xi * per_corner, 0, per_corner - 1)
    seg_ids = jnp.clip(tile_coords[:, 2] - seg_i * (held * nz), 0, held * nz - 1)
    match = tile_coords[:, 1][:, None] == owner_map[None, :]
    slot = jnp.sum(jnp.where(match, jnp.arange(owner_map.shape[0], dtype=jnp.int32)[None, :], 0), axis=1)
    place = (slot // (2 * nx)) * nx + slot % nx
    live = jnp.arange(tiles, dtype=jnp.int32) < tile_count[0]
    here = (slot // nx) % 2 == core
    keep_ids = jnp.where(live & here, place, owners)
    send_ids = jnp.where(live & jnp.logical_not(here), place, owners)

    blocks = gathered.reshape(-1, seg_width, cols)

    def seg_spec(g):
        return pl.BlockSpec((1, seg_width, cols), lambda t, ids, *_: (ids[t * GRP + g], 0, 0))

    keep, send = pl.pallas_call(
        contract_kernel,
        grid_spec=pltpu.PrefetchScalarGridSpec(
            num_scalar_prefetch=4,
            grid=(tiles // GRP,),
            in_specs=[
                pl.BlockSpec((GRP, net_rows, width), lambda t, *_: (t, 0, 0)),
                *[seg_spec(g) for g in range(GRP)],
                pl.BlockSpec((per_corner, CBLK, cols), lambda t, *_: (0, 0, 0)),
            ],
            out_specs=[
                pl.BlockSpec((owners + 1, net_rows, cols), lambda t, *_: (0, 0, 0)),
                pl.BlockSpec((owners + 1, net_rows, cols), lambda t, *_: (0, 0, 0)),
            ],
        ),
        out_shape=[jax.ShapeDtypeStruct((owners + 1, net_rows, cols), jnp.float32)] * 2,
        compiler_params=pltpu.CompilerParams(vmem_limit_bytes=48 << 20),
        name="contract",
    )(
        seg_ids,
        corner_ids,
        keep_ids,
        send_ids,
        tile_values,
        *[blocks] * GRP,
        corner_factor.reshape(per_corner, CBLK, cols),
    )
    received = lax.ppermute(send, "core", [(0, 1), (1, 0)])
    solved = pl.pallas_call(
        whiten_kernel,
        out_shape=jax.ShapeDtypeStruct((owners, net_rows, cols), jnp.bfloat16),
        compiler_params=pltpu.CompilerParams(vmem_limit_bytes=32 << 20),
        name="apply_inverse",
    )(keep, received, inverse)
    shares = lax.all_to_all(solved, ("y", "corner"), 0, 0)
    return jnp.sum(shares.astype(jnp.float32), axis=0)


def solution(mesh):
    nz, seg, nx = mesh.devices.shape
    split = Mesh(mesh.devices.reshape(4, nz // 4, seg // 2, 2, nx), ALL)
    return jax.shard_map(
        body,
        mesh=split,
        in_specs=(
            P(ALL, None, None),
            P(ALL, None),
            P(ALL),
            P(NET),
            P("corner", None),
            P(SEG + NET, None),
        ),
        out_specs=P(ALL, None),
        check_vma=False,
    )
```

```python
import functools

import jax
import jax.numpy as jnp
from jax import lax
from jax.experimental import pallas as pl
from jax.experimental.pallas import tpu as pltpu
from jax.sharding import Mesh, PartitionSpec as P

CBLK = 8
CAP = 2
PIVOTS = 4
GRP = 8
NET = ("zh", "zl")
SEG = ("y", "core")
PLANE = SEG + ("corner",)
ALL = NET + PLANE
FREE = pl.CostEstimate(flops=0, transcendentals=0, bytes_accessed=0)
HIGH = lax.Precision.HIGHEST


def mm(a, b):
    return jnp.dot(a, b, precision=HIGH, preferred_element_type=jnp.float32)


def invert_pivot(p):
    m = len(p)
    if m == 2:
        inv = 1.0 / (p[0][0] * p[1][1] - p[0][1] * p[0][1])
        off = -p[0][1] * inv
        return [[p[1][1] * inv, off], [off, p[0][0] * inv]]
    h = m // 2
    r = range(h)
    ai = invert_pivot([row[:h] for row in p[:h]])
    b = [row[h:] for row in p[:h]]
    w = [[sum(ai[i][l] * b[l][j] for l in r) for j in r] for i in r]
    s = [[p[h + i][h + j] - sum(b[l][min(i, j)] * w[l][max(i, j)] for l in r) for j in r] for i in r]
    q = invert_pivot(s)
    wq = [[sum(w[i][l] * q[l][j] for l in r) for j in r] for i in r]
    top = [[ai[i][j] + sum(wq[i][l] * w[j][l] for l in r) for j in r] for i in r]
    return [top[i] + [-x for x in wq[i]] for i in r] + [[-wq[j][i] for j in r] + q[i] for i in r]


def invert_block(a):
    n = a.shape[0]
    m = PIVOTS
    lane = lax.broadcasted_iota(jnp.int32, (1, n), 1)
    sub = lax.broadcasted_iota(jnp.int32, (n, 1), 0)
    for k in range(0, n, m):
        rows = [a[k + i : k + i + 1, :] for i in range(m)]
        p = [[None] * m for _ in range(m)]
        for i in range(m):
            for j in range(i, m):
                p[i][j] = p[j][i] = jnp.broadcast_to(rows[i][:, k + j : k + j + 1], (1, n))
        q = invert_pivot(p)
        in_lane = (lane >= k) & (lane < k + m)
        in_sub = (sub >= k) & (sub < k + m)
        new = jnp.where(in_lane | in_sub, 0.0, a)
        for i in range(m):
            row = sum(q[i][j] * rows[j] for j in range(m))
            for j in range(m):
                row = jnp.where(lane == k + j, q[i][j], row)
            col = jnp.where(in_sub, jnp.where(sub == k + i, -1.0, 0.0), a[:, k + i : k + i + 1])
            new = new - col * row
        a = new
    return a


def split(x):
    high = x.astype(jnp.bfloat16)
    return high, (x - high.astype(jnp.float32)).astype(jnp.bfloat16)


def product(a, b):
    out = jnp.dot(a[0], b[1], preferred_element_type=jnp.float32)
    out += jnp.dot(a[1], b[0], preferred_element_type=jnp.float32)
    return out + jnp.dot(a[0], b[0], preferred_element_type=jnp.float32)


def prepare_kernel(coords_ref, seg_ref, corner_ref, slot_ref, out_ref, *, held, holders, near):
    xi = lax.axis_index("corner")
    seg_i = lax.axis_index("y") * lax.axis_size("core") + lax.axis_index("core")
    cols = seg_ref.shape[1]
    seg = seg_ref[...]
    gram = lax.dot_general(seg, seg, (((0,), (0,)), ((), ())), preferred_element_type=jnp.float32)
    lane = lax.broadcasted_iota(jnp.int32, (1, cols), 1)
    rows = [jnp.zeros((1, cols), jnp.float32) for _ in range(near)]
    seen = []
    for t in range(coords_ref.shape[0]):
        local = jnp.clip(coords_ref[t, 2] - seg_i * (held * holders), 0, held * holders - 1)
        holder = local // held
        rank = jnp.int32(0)
        for other in seen:
            rank += (other == holder).astype(jnp.int32)
        rank = jnp.minimum(rank, CAP - 1)
        seen.append(holder)
        place = holder * CAP + rank
        shift = lax.rem(xi - holder // near + near, near)
        slot_ref[t] = shift * (near * CAP) + (holder % near) * CAP + rank
        for c in range(near):
            rows[c] = jnp.where(lane == place - c * near * CAP, (local % held).astype(jnp.float32), rows[c])
    corner = corner_ref[...].astype(jnp.float32)
    nseg = out_ref.shape[0] // near
    per = corner.shape[0] // nseg
    own = jnp.zeros((per, cols), jnp.float32)
    for s in range(nseg):
        own = jnp.where(seg_i == s, corner[s * per : (s + 1) * per], own)
    split_rows = 8 // near
    gram = gram.reshape(out_ref.shape[0], 8, cols)
    piece = jnp.zeros((out_ref.shape[0], split_rows, cols), jnp.float32)
    for c in range(near):
        piece = jnp.where(xi == c, gram[:, c * split_rows : (c + 1) * split_rows], piece)
    pad = jnp.zeros((8 - split_rows - 1 - per, cols), jnp.float32)
    for p in range(out_ref.shape[0]):
        out_ref[p] = jnp.concatenate([piece[p], rows[p % near], own, pad], axis=0)


def select_kernel(req_ref, *refs):
    hold = len(refs) // 2
    parts, outs = refs[:hold], refs[hold:]
    zl = lax.axis_index("zl")
    xi = lax.axis_index("corner")
    for offset in range(hold):
        residue = lax.rem(zl + offset, hold)
        for shift in range(hold):
            dest = lax.rem(xi + shift, hold)
            for rank in range(CAP):
                slot = residue * CAP + rank
                outs[shift][slot] = parts[offset][req_ref[dest, slot]]


def scale_kernel(corner_ref, out_ref):
    corner = corner_ref[...]
    n, cols = corner.shape
    wide = jnp.concatenate([corner, jnp.zeros((128 - n, cols), jnp.float32)], axis=0) if n < 128 else corner
    n = wide.shape[0]
    d = 1.0 / jnp.sum(wide * wide, axis=0, keepdims=True)
    scaled = wide * d
    eye = lax.broadcasted_iota(jnp.int32, (n, n), 0) == lax.broadcasted_iota(jnp.int32, (n, n), 1)
    inner = jnp.where(eye, 1.0, 0.0) + lax.dot_general(
        scaled, wide, (((1,), (1,)), ((), ())), precision=HIGH, preferred_element_type=jnp.float32
    )
    small = mm(invert_block(inner), scaled)
    low = lax.dot_general(
        scaled, small, (((0,), (0,)), ((), ())), precision=HIGH, preferred_element_type=jnp.float32
    )
    diag = lax.broadcasted_iota(jnp.int32, (cols, cols), 0) == lax.broadcasted_iota(jnp.int32, (cols, cols), 1)
    out_ref[...] = jnp.where(diag, d, 0.0) - low


def contract_kernel(seg_ids, corner_ids, keep_ids, send_ids, values_ref, *refs):
    seg_refs, (corner_ref, keep_ref, send_ref) = refs[:-3], refs[-3:]
    per = seg_refs[0].shape[0]
    step = pl.program_id(0)

    @pl.when(step == 0)
    def _():
        keep_ref[...] = jnp.zeros_like(keep_ref)
        send_ref[...] = jnp.zeros_like(send_ref)

    for g in range(values_ref.shape[0]):
        t = step * values_ref.shape[0] + g
        at = lax.rem(seg_ids[t], per)
        source = seg_ids[t] // per
        seg_rows = seg_refs[0][at]
        for k in range(1, len(seg_refs)):
            seg_rows = jnp.where(source == k, seg_refs[k][at], seg_rows)
        seg_rows = seg_rows.astype(jnp.float32)
        corner_rows = corner_ref[corner_ids[t]].astype(jnp.float32)
        khatri = jnp.concatenate(
            [(corner_rows[a : a + 1, :] * seg_rows).astype(jnp.bfloat16) for a in range(CBLK)], axis=0
        )
        part = jnp.dot(values_ref[g], khatri, preferred_element_type=jnp.float32)
        keep_ref[keep_ids[t]] += part
        send_ref[send_ids[t]] += part


def scaled_kernel(keep_ref, recv_ref, scale_ref, out_ref):
    scale = split(scale_ref[...])

    def block(i, carry):
        out_ref[i] = product(split(keep_ref[i] + recv_ref[i]), scale).astype(jnp.bfloat16)
        return carry

    lax.fori_loop(0, out_ref.shape[0], block, 0, unroll=4)


def inverse_kernel(seg_gram_ref, corner_ref, out_ref):
    cols = out_ref.shape[1]
    corner = corner_ref[...]
    low = corner.astype(jnp.bfloat16)
    corner_gram = lax.dot_general(low, low, (((0,), (0,)), ((), ())), preferred_element_type=jnp.float32)
    gram = seg_gram_ref[...].reshape(cols, cols) * corner_gram
    h = cols // 2
    a12 = gram[:h, h:]
    a21 = gram[h:, :h]
    p = invert_block(gram[:h, :h])
    w = mm(p, a12)
    v = mm(a21, p)
    q = invert_block(gram[h:, h:] - mm(a21, w))
    wq = mm(w, q)
    top = jnp.concatenate([p + mm(wq, v), -wq], axis=1)
    bottom = jnp.concatenate([-mm(q, v), q], axis=1)
    inverse = jnp.concatenate([top, bottom], axis=0)
    diag = lax.broadcasted_iota(jnp.int32, (cols, cols), 0) == lax.broadcasted_iota(jnp.int32, (cols, cols), 1)
    d = jnp.sum(corner * corner, axis=0, keepdims=True)
    out_ref[...] = mm(corner_gram + jnp.where(diag, d, 0.0), inverse)


def final_kernel(shares_ref, right_ref, out_ref):
    total = shares_ref[0].astype(jnp.float32)
    for i in range(1, shares_ref.shape[0]):
        total += shares_ref[i].astype(jnp.float32)
    out_ref[...] = product(split(total), split(right_ref[...]))


def call(kernel, name, out_shape, in_specs, out_specs, *operands, scratch=()):
    return pl.pallas_call(
        kernel,
        in_specs=in_specs,
        out_specs=out_specs,
        out_shape=out_shape,
        scratch_shapes=scratch,
        compiler_params=pltpu.CompilerParams(vmem_limit_bytes=32 << 20),
        cost_estimate=FREE,
        name=name,
    )(*operands)


def body(tile_values, tile_coords, tile_count, owner_map, corner_factor, seg_factor):
    tiles, net_rows, width = tile_values.shape
    cols = corner_factor.shape[1]
    seg_width = width // CBLK
    nz = lax.axis_size(NET)
    nx = lax.axis_size("corner")
    nseg = lax.axis_size(SEG)
    core = lax.axis_index("core")
    xi = lax.axis_index("corner")
    seg_i = lax.axis_index(SEG)
    per_corner = corner_factor.shape[0] // CBLK
    held = seg_factor.shape[0] // seg_width
    owners = lax.axis_size("y") * nx
    near = nz // nx
    f32 = functools.partial(jax.ShapeDtypeStruct, dtype=jnp.float32)
    smem = pl.BlockSpec(memory_space=pltpu.SMEM)
    vmem = pl.BlockSpec(memory_space=pltpu.VMEM)

    far = [
        (h * nx + x, (h + near * ((x + h) % nx)) % nz * nx + h // near)
        for h in range(nz)
        for x in range(nx)
    ]
    own_rows = lax.ppermute(seg_factor, NET + ("corner",), far)
    slot_of, packet = call(
        functools.partial(prepare_kernel, held=held, holders=nz, near=near),
        "prepare",
        [jax.ShapeDtypeStruct((tiles,), jnp.int32), f32((nseg * nx, 8, cols))],
        [smem, vmem, vmem],
        [smem, vmem],
        tile_coords,
        seg_factor,
        corner_factor,
    )
    packet = lax.all_to_all(packet, PLANE, 0, 0)
    own_rows, packet = lax.optimization_barrier((own_rows, packet))
    up = lax.ppermute(own_rows, NET, [((z + 1) % nz, z) for z in range(nz)])
    two = lax.ppermute(own_rows, NET, [((z + (2 if z % 2 else -2)) % nz, z) for z in range(nz)])
    down = lax.ppermute(own_rows, NET, [((z - 1) % nz, z) for z in range(nz)])
    packet = packet.reshape(nseg, nx, 8, cols)
    cut = 8 // nx
    corner_all = packet[:, :, cut + 1 : cut + 1 + corner_factor.shape[0] // nseg].reshape(-1, cols)
    request = lax.dynamic_index_in_dim(packet[:, :, cut, : near * CAP], seg_i, 0, keepdims=False)
    request = jnp.clip(request.astype(jnp.int32), 0, held - 1)
    chunk = jnp.sum(packet[:, :, :cut], axis=0).reshape(8, cols)
    chunk = jnp.sum(lax.all_to_all(jnp.broadcast_to(chunk[None], (nz // near, 8, cols)), "zh", 0, 0), axis=0)
    up, two, down, chunk, request = lax.optimization_barrier((up, two, down, chunk, request))
    chosen = call(
        select_kernel,
        "select_blocks",
        [jax.ShapeDtypeStruct((near * CAP, seg_width, cols), seg_factor.dtype)] * nx,
        [smem] + [vmem] * near,
        [vmem] * nx,
        request,
        *(v.reshape(held, seg_width, cols) for v in (own_rows, up, two, down)),
    )
    blocks = [chosen[0]] + [
        lax.ppermute(chosen[k], "corner", [(x, (x + k) % nx) for x in range(nx)]) for k in range(1, nx)
    ]
    chunk, corner_all = lax.optimization_barrier((chunk, corner_all))
    scale = call(scale_kernel, "corner_scale", f32((cols, cols)), [vmem], vmem, corner_all)
    chunk = jnp.sum(lax.all_to_all(jnp.broadcast_to(chunk[None], (near, 8, cols)), "zl", 0, 0), axis=0)
    seg_gram = lax.all_to_all(jnp.broadcast_to(chunk[None], (nseg * nx, 8, cols)), PLANE, 0, 0)
    blocks, seg_gram, scale = lax.optimization_barrier((blocks, seg_gram, scale))

    corner_ids = jnp.clip(tile_coords[:, 0] - xi * per_corner, 0, per_corner - 1)
    match = tile_coords[:, 1][:, None] == owner_map[None, :]
    slot = jnp.sum(jnp.where(match, jnp.arange(owner_map.shape[0], dtype=jnp.int32)[None, :], 0), axis=1)
    place = (slot // (2 * nx)) * nx + slot % nx
    live = jnp.arange(tiles, dtype=jnp.int32) < tile_count[0]
    here = (slot // nx) % 2 == core
    keep_ids = jnp.where(live & here, place, owners)
    send_ids = jnp.where(live & jnp.logical_not(here), place, owners)
    keep, send = pl.pallas_call(
        contract_kernel,
        grid_spec=pltpu.PrefetchScalarGridSpec(
            num_scalar_prefetch=4,
            grid=(tiles // GRP,),
            in_specs=[pl.BlockSpec((GRP, net_rows, width), lambda t, *_: (t, 0, 0))]
            + [vmem] * nx
            + [pl.BlockSpec((per_corner, CBLK, cols), lambda t, *_: (0, 0, 0))],
            out_specs=[pl.BlockSpec((owners + 1, net_rows, cols), lambda t, *_: (0, 0, 0))] * 2,
        ),
        out_shape=[f32((owners + 1, net_rows, cols))] * 2,
        compiler_params=pltpu.CompilerParams(vmem_limit_bytes=48 << 20),
        name="contract",
    )(
        slot_of,
        corner_ids,
        keep_ids,
        send_ids,
        tile_values,
        *blocks,
        corner_factor.reshape(per_corner, CBLK, cols),
    )
    received = lax.ppermute(send, "core", [(0, 1), (1, 0)])
    solved = call(
        scaled_kernel,
        "apply_scale",
        jax.ShapeDtypeStruct((owners, net_rows, cols), jnp.bfloat16),
        [vmem] * 3,
        vmem,
        keep,
        received,
        scale,
    )
    solved, seg_gram = lax.optimization_barrier((solved, seg_gram))
    shares = lax.all_to_all(solved, ("y", "corner"), 0, 0)
    right = call(inverse_kernel, "gram_inverse", f32((cols, cols)), [vmem] * 2, vmem, seg_gram, corner_all)
    return call(final_kernel, "final", f32((net_rows, cols)), [vmem] * 2, vmem, shares, right)


def solution(mesh):
    nz, seg, nx = mesh.devices.shape
    axes = Mesh(mesh.devices.reshape(nx, nz // nx, seg // 2, 2, nx), ALL)
    return jax.shard_map(
        body,
        mesh=axes,
        in_specs=(
            P(ALL, None, None),
            P(ALL, None),
            P(ALL),
            P(NET),
            P("corner", None),
            P(SEG + NET, None),
        ),
        out_specs=P(ALL, None),
        check_vma=False,
    )
```

```python
import functools

import jax
import jax.numpy as jnp
from jax import lax
from jax.experimental import pallas as pl
from jax.experimental.pallas import tpu as pltpu
from jax.sharding import Mesh, PartitionSpec as P

CBLK = 8
CAP = 2
PIVOTS = 4
GRP = 8
NET = ("zh", "zl")
SEG = ("y", "core")
PLANE = SEG + ("corner",)
ALL = NET + PLANE
FREE = pl.CostEstimate(flops=0, transcendentals=0, bytes_accessed=0)
HIGH = lax.Precision.HIGHEST


def mm(a, b):
    return jnp.dot(a, b, precision=HIGH, preferred_element_type=jnp.float32)


def invert_pivot(p):
    m = len(p)
    if m == 2:
        inv = 1.0 / (p[0][0] * p[1][1] - p[0][1] * p[0][1])
        off = -p[0][1] * inv
        return [[p[1][1] * inv, off], [off, p[0][0] * inv]]
    h = m // 2
    r = range(h)
    ai = invert_pivot([row[:h] for row in p[:h]])
    b = [row[h:] for row in p[:h]]
    w = [[sum(ai[i][l] * b[l][j] for l in r) for j in r] for i in r]
    s = [[p[h + i][h + j] - sum(b[l][min(i, j)] * w[l][max(i, j)] for l in r) for j in r] for i in r]
    q = invert_pivot(s)
    wq = [[sum(w[i][l] * q[l][j] for l in r) for j in r] for i in r]
    top = [[ai[i][j] + sum(wq[i][l] * w[j][l] for l in r) for j in r] for i in r]
    return [top[i] + [-x for x in wq[i]] for i in r] + [[-wq[j][i] for j in r] + q[i] for i in r]


def invert_block(a):
    n = a.shape[0]
    m = PIVOTS
    lane = lax.broadcasted_iota(jnp.int32, (1, n), 1)
    sub = lax.broadcasted_iota(jnp.int32, (n, 1), 0)
    for k in range(0, n, m):
        rows = [a[k + i : k + i + 1, :] for i in range(m)]
        p = [[None] * m for _ in range(m)]
        for i in range(m):
            for j in range(i, m):
                p[i][j] = p[j][i] = jnp.broadcast_to(rows[i][:, k + j : k + j + 1], (1, n))
        q = invert_pivot(p)
        in_lane = (lane >= k) & (lane < k + m)
        in_sub = (sub >= k) & (sub < k + m)
        new = jnp.where(in_lane | in_sub, 0.0, a)
        for i in range(m):
            row = sum(q[i][j] * rows[j] for j in range(m))
            for j in range(m):
                row = jnp.where(lane == k + j, q[i][j], row)
            col = jnp.where(in_sub, jnp.where(sub == k + i, -1.0, 0.0), a[:, k + i : k + i + 1])
            new = new - col * row
        a = new
    return a


def split(x):
    high = x.astype(jnp.bfloat16)
    return high, (x - high.astype(jnp.float32)).astype(jnp.bfloat16)


def product(a, b):
    out = jnp.dot(a[0], b[1], preferred_element_type=jnp.float32)
    out += jnp.dot(a[1], b[0], preferred_element_type=jnp.float32)
    return out + jnp.dot(a[0], b[0], preferred_element_type=jnp.float32)


def prepare_kernel(coords_ref, seg_ref, corner_ref, slot_ref, out_ref, *, held, holders, near):
    xi = lax.axis_index("corner")
    seg_i = lax.axis_index("y") * lax.axis_size("core") + lax.axis_index("core")
    cols = seg_ref.shape[1]
    seg = seg_ref[...]
    gram = lax.dot_general(seg, seg, (((0,), (0,)), ((), ())), preferred_element_type=jnp.float32)
    lane = lax.broadcasted_iota(jnp.int32, (1, cols), 1)
    rows = [jnp.zeros((1, cols), jnp.float32) for _ in range(near)]
    seen = []
    for t in range(coords_ref.shape[0]):
        local = jnp.clip(coords_ref[t, 2] - seg_i * (held * holders), 0, held * holders - 1)
        holder = local // held
        rank = jnp.int32(0)
        for other in seen:
            rank += (other == holder).astype(jnp.int32)
        rank = jnp.minimum(rank, CAP - 1)
        seen.append(holder)
        place = holder * CAP + rank
        shift = lax.rem(xi - holder // near + near, near)
        slot_ref[t] = shift * (near * CAP) + (holder % near) * CAP + rank
        for c in range(near):
            rows[c] = jnp.where(lane == place - c * near * CAP, (local % held).astype(jnp.float32), rows[c])
    corner = corner_ref[...].astype(jnp.float32)
    nseg = out_ref.shape[0] // near
    per = corner.shape[0] // nseg
    own = jnp.zeros((per, cols), jnp.float32)
    for s in range(nseg):
        own = jnp.where(seg_i == s, corner[s * per : (s + 1) * per], own)
    split_rows = 8 // near
    gram = gram.reshape(out_ref.shape[0], 8, cols)
    piece = jnp.zeros((out_ref.shape[0], split_rows, cols), jnp.float32)
    for c in range(near):
        piece = jnp.where(xi == c, gram[:, c * split_rows : (c + 1) * split_rows], piece)
    pad = jnp.zeros((8 - split_rows - 1 - per, cols), jnp.float32)
    for p in range(out_ref.shape[0]):
        out_ref[p] = jnp.concatenate([piece[p], rows[p % near], own, pad], axis=0)


def select_kernel(req_ref, *refs):
    hold = len(refs) // 2
    parts, outs = refs[:hold], refs[hold:]
    zl = lax.axis_index("zl")
    xi = lax.axis_index("corner")
    for offset in range(hold):
        residue = lax.rem(zl + offset, hold)
        for shift in range(hold):
            dest = lax.rem(xi + shift, hold)
            for rank in range(CAP):
                slot = residue * CAP + rank
                outs[shift][slot] = parts[offset][req_ref[dest, slot]]


def scale_kernel(corner_ref, out_ref):
    corner = corner_ref[...]
    n, cols = corner.shape
    wide = jnp.concatenate([corner, jnp.zeros((128 - n, cols), jnp.float32)], axis=0) if n < 128 else corner
    n = wide.shape[0]
    d = 1.0 / jnp.sum(wide * wide, axis=0, keepdims=True)
    scaled = wide * d
    eye = lax.broadcasted_iota(jnp.int32, (n, n), 0) == lax.broadcasted_iota(jnp.int32, (n, n), 1)
    inner = jnp.where(eye, 1.0, 0.0) + lax.dot_general(
        scaled, wide, (((1,), (1,)), ((), ())), precision=HIGH, preferred_element_type=jnp.float32
    )
    small = mm(invert_block(inner), scaled)
    low = lax.dot_general(
        scaled, small, (((0,), (0,)), ((), ())), precision=HIGH, preferred_element_type=jnp.float32
    )
    diag = lax.broadcasted_iota(jnp.int32, (cols, cols), 0) == lax.broadcasted_iota(jnp.int32, (cols, cols), 1)
    out_ref[...] = jnp.where(diag, d, 0.0) - low


def contract_kernel(seg_ids, corner_ids, keep_ids, send_ids, values_ref, *refs):
    seg_refs, (corner_ref, keep_ref, send_ref) = refs[:-3], refs[-3:]
    per = seg_refs[0].shape[0]
    step = pl.program_id(0)

    @pl.when(step == 0)
    def _():
        keep_ref[...] = jnp.zeros_like(keep_ref)
        send_ref[...] = jnp.zeros_like(send_ref)

    for g in range(values_ref.shape[0]):
        t = step * values_ref.shape[0] + g
        at = lax.rem(seg_ids[t], per)
        source = seg_ids[t] // per
        seg_rows = seg_refs[0][at]
        for k in range(1, len(seg_refs)):
            seg_rows = jnp.where(source == k, seg_refs[k][at], seg_rows)
        seg_rows = seg_rows.astype(jnp.float32)
        corner_rows = corner_ref[corner_ids[t]].astype(jnp.float32)
        khatri = jnp.concatenate(
            [(corner_rows[a : a + 1, :] * seg_rows).astype(jnp.bfloat16) for a in range(CBLK)], axis=0
        )
        part = jnp.dot(values_ref[g], khatri, preferred_element_type=jnp.float32)
        keep_ref[keep_ids[t]] += part
        send_ref[send_ids[t]] += part


def scaled_kernel(keep_ref, recv_ref, scale_ref, out_ref):
    scale = split(scale_ref[...])

    def block(i, carry):
        out_ref[i] = product(split(keep_ref[i] + recv_ref[i]), scale).astype(jnp.bfloat16)
        return carry

    lax.fori_loop(0, out_ref.shape[0], block, 0, unroll=4)


def inverse_kernel(seg_gram_ref, corner_ref, out_ref):
    cols = out_ref.shape[1]
    corner = corner_ref[...]
    low = corner.astype(jnp.bfloat16)
    corner_gram = lax.dot_general(low, low, (((0,), (0,)), ((), ())), preferred_element_type=jnp.float32)
    gram = seg_gram_ref[...].reshape(cols, cols) * corner_gram
    h = cols // 2
    a12 = gram[:h, h:]
    a21 = gram[h:, :h]
    p = invert_block(gram[:h, :h])
    w = mm(p, a12)
    v = mm(a21, p)
    q = invert_block(gram[h:, h:] - mm(a21, w))
    wq = mm(w, q)
    top = jnp.concatenate([p + mm(wq, v), -wq], axis=1)
    bottom = jnp.concatenate([-mm(q, v), q], axis=1)
    inverse = jnp.concatenate([top, bottom], axis=0)
    diag = lax.broadcasted_iota(jnp.int32, (cols, cols), 0) == lax.broadcasted_iota(jnp.int32, (cols, cols), 1)
    d = jnp.sum(corner * corner, axis=0, keepdims=True)
    out_ref[...] = mm(corner_gram + jnp.where(diag, d, 0.0), inverse)


def final_kernel(shares_ref, right_ref, out_ref):
    total = shares_ref[0].astype(jnp.float32)
    for i in range(1, shares_ref.shape[0]):
        total += shares_ref[i].astype(jnp.float32)
    out_ref[...] = product(split(total), split(right_ref[...]))


def call(kernel, name, out_shape, in_specs, out_specs, *operands, scratch=()):
    return pl.pallas_call(
        kernel,
        in_specs=in_specs,
        out_specs=out_specs,
        out_shape=out_shape,
        scratch_shapes=scratch,
        compiler_params=pltpu.CompilerParams(vmem_limit_bytes=32 << 20),
        cost_estimate=FREE,
        name=name,
    )(*operands)


def body(tile_values, tile_coords, tile_count, owner_map, corner_factor, seg_factor):
    tiles, net_rows, width = tile_values.shape
    cols = corner_factor.shape[1]
    seg_width = width // CBLK
    nz = lax.axis_size(NET)
    nx = lax.axis_size("corner")
    nseg = lax.axis_size(SEG)
    core = lax.axis_index("core")
    xi = lax.axis_index("corner")
    seg_i = lax.axis_index(SEG)
    per_corner = corner_factor.shape[0] // CBLK
    held = seg_factor.shape[0] // seg_width
    owners = lax.axis_size("y") * nx
    near = nz // nx
    f32 = functools.partial(jax.ShapeDtypeStruct, dtype=jnp.float32)
    smem = pl.BlockSpec(memory_space=pltpu.SMEM)
    vmem = pl.BlockSpec(memory_space=pltpu.VMEM)

    far = [
        (h * nx + x, (h + near * ((x + h) % nx)) % nz * nx + h // near)
        for h in range(nz)
        for x in range(nx)
    ]
    own_rows = lax.ppermute(seg_factor, NET + ("corner",), far)
    slot_of, packet = call(
        functools.partial(prepare_kernel, held=held, holders=nz, near=near),
        "prepare",
        [jax.ShapeDtypeStruct((tiles,), jnp.int32), f32((nseg * nx, 8, cols))],
        [smem, vmem, vmem],
        [smem, vmem],
        tile_coords,
        seg_factor,
        corner_factor,
    )
    packet = lax.all_to_all(packet, PLANE, 0, 0)
    own_rows, packet = lax.optimization_barrier((own_rows, packet))
    up = lax.ppermute(own_rows, NET, [((z + 1) % nz, z) for z in range(nz)])
    two = lax.ppermute(own_rows, NET, [((z + (2 if z % 2 else -2)) % nz, z) for z in range(nz)])
    down = lax.ppermute(own_rows, NET, [((z - 1) % nz, z) for z in range(nz)])
    packet = packet.reshape(nseg, nx, 8, cols)
    cut = 8 // nx
    corner_all = packet[:, :, cut + 1 : cut + 1 + corner_factor.shape[0] // nseg].reshape(-1, cols)
    request = lax.dynamic_index_in_dim(packet[:, :, cut, : near * CAP], seg_i, 0, keepdims=False)
    request = jnp.clip(request.astype(jnp.int32), 0, held - 1)
    chunk = jnp.sum(packet[:, :, :cut], axis=0).reshape(8, cols)
    chunk = jnp.sum(lax.all_to_all(jnp.broadcast_to(chunk[None], (near, 8, cols)), "zl", 0, 0), axis=0)
    up, two, down, chunk, request = lax.optimization_barrier((up, two, down, chunk, request))
    chosen = call(
        select_kernel,
        "select_blocks",
        [jax.ShapeDtypeStruct((near * CAP, seg_width, cols), seg_factor.dtype)] * nx,
        [smem] + [vmem] * near,
        [vmem] * nx,
        request,
        *(v.reshape(held, seg_width, cols) for v in (own_rows, up, two, down)),
    )
    _, chunk, corner_all = lax.optimization_barrier((chosen[1], chunk, corner_all))
    blocks = [chosen[0]] + [
        lax.ppermute(chosen[k], "corner", [(x, (x + k) % nx) for x in range(nx)]) for k in range(1, nx)
    ]
    scale = call(scale_kernel, "corner_scale", f32((cols, cols)), [vmem], vmem, corner_all)
    chunk = jnp.sum(lax.all_to_all(jnp.broadcast_to(chunk[None], (nz // near, 8, cols)), "zh", 0, 0), axis=0)
    seg_gram = lax.all_to_all(jnp.broadcast_to(chunk[None], (nseg * nx, 8, cols)), PLANE, 0, 0)
    blocks, seg_gram, scale = lax.optimization_barrier((blocks, seg_gram, scale))

    corner_ids = jnp.clip(tile_coords[:, 0] - xi * per_corner, 0, per_corner - 1)
    match = tile_coords[:, 1][:, None] == owner_map[None, :]
    slot = jnp.sum(jnp.where(match, jnp.arange(owner_map.shape[0], dtype=jnp.int32)[None, :], 0), axis=1)
    place = (slot // (2 * nx)) * nx + slot % nx
    live = jnp.arange(tiles, dtype=jnp.int32) < tile_count[0]
    here = (slot // nx) % 2 == core
    keep_ids = jnp.where(live & here, place, owners)
    send_ids = jnp.where(live & jnp.logical_not(here), place, owners)
    keep, send = pl.pallas_call(
        contract_kernel,
        grid_spec=pltpu.PrefetchScalarGridSpec(
            num_scalar_prefetch=4,
            grid=(tiles // GRP,),
            in_specs=[pl.BlockSpec((GRP, net_rows, width), lambda t, *_: (t, 0, 0))]
            + [vmem] * nx
            + [pl.BlockSpec((per_corner, CBLK, cols), lambda t, *_: (0, 0, 0))],
            out_specs=[pl.BlockSpec((owners + 1, net_rows, cols), lambda t, *_: (0, 0, 0))] * 2,
        ),
        out_shape=[f32((owners + 1, net_rows, cols))] * 2,
        compiler_params=pltpu.CompilerParams(vmem_limit_bytes=48 << 20),
        name="contract",
    )(
        slot_of,
        corner_ids,
        keep_ids,
        send_ids,
        tile_values,
        *blocks,
        corner_factor.reshape(per_corner, CBLK, cols),
    )
    received = lax.ppermute(send, "core", [(0, 1), (1, 0)])
    solved = call(
        scaled_kernel,
        "apply_scale",
        jax.ShapeDtypeStruct((owners, net_rows, cols), jnp.bfloat16),
        [vmem] * 3,
        vmem,
        keep,
        received,
        scale,
    )
    solved, seg_gram = lax.optimization_barrier((solved, seg_gram))
    shares = lax.all_to_all(solved, ("y", "corner"), 0, 0)
    right = call(inverse_kernel, "gram_inverse", f32((cols, cols)), [vmem] * 2, vmem, seg_gram, corner_all)
    return call(final_kernel, "final", f32((net_rows, cols)), [vmem] * 2, vmem, shares, right)


def solution(mesh):
    nz, seg, nx = mesh.devices.shape
    axes = Mesh(mesh.devices.reshape(nx, nz // nx, seg // 2, 2, nx), ALL)
    return jax.shard_map(
        body,
        mesh=axes,
        in_specs=(
            P(ALL, None, None),
            P(ALL, None),
            P(ALL),
            P(NET),
            P("corner", None),
            P(SEG + NET, None),
        ),
        out_specs=P(ALL, None),
        check_vma=False,
    )
```

```python
import functools

import jax
import jax.numpy as jnp
from jax import lax
from jax.experimental import pallas as pl
from jax.experimental.pallas import tpu as pltpu
from jax.sharding import Mesh, PartitionSpec as P

CBLK = 8
CAP = 2
PIVOTS = 4
GRP = 8
NET = ("zh", "zl")
SEG = ("y", "core")
PLANE = SEG + ("corner",)
ALL = NET + PLANE
FREE = pl.CostEstimate(flops=0, transcendentals=0, bytes_accessed=0)
HIGH = lax.Precision.HIGHEST


def mm(a, b):
    return jnp.dot(a, b, precision=HIGH, preferred_element_type=jnp.float32)


def invert_pivot(p):
    m = len(p)
    if m == 2:
        inv = 1.0 / (p[0][0] * p[1][1] - p[0][1] * p[0][1])
        off = -p[0][1] * inv
        return [[p[1][1] * inv, off], [off, p[0][0] * inv]]
    h = m // 2
    r = range(h)
    ai = invert_pivot([row[:h] for row in p[:h]])
    b = [row[h:] for row in p[:h]]
    w = [[sum(ai[i][l] * b[l][j] for l in r) for j in r] for i in r]
    s = [[p[h + i][h + j] - sum(b[l][min(i, j)] * w[l][max(i, j)] for l in r) for j in r] for i in r]
    q = invert_pivot(s)
    wq = [[sum(w[i][l] * q[l][j] for l in r) for j in r] for i in r]
    top = [[ai[i][j] + sum(wq[i][l] * w[j][l] for l in r) for j in r] for i in r]
    return [top[i] + [-x for x in wq[i]] for i in r] + [[-wq[j][i] for j in r] + q[i] for i in r]


def invert_block(a):
    n = a.shape[0]
    m = PIVOTS
    lane = lax.broadcasted_iota(jnp.int32, (1, n), 1)
    sub = lax.broadcasted_iota(jnp.int32, (n, 1), 0)
    for k in range(0, n, m):
        rows = [a[k + i : k + i + 1, :] for i in range(m)]
        p = [[None] * m for _ in range(m)]
        for i in range(m):
            for j in range(i, m):
                p[i][j] = p[j][i] = jnp.broadcast_to(rows[i][:, k + j : k + j + 1], (1, n))
        q = invert_pivot(p)
        in_lane = (lane >= k) & (lane < k + m)
        in_sub = (sub >= k) & (sub < k + m)
        new = jnp.where(in_lane | in_sub, 0.0, a)
        for i in range(m):
            row = sum(q[i][j] * rows[j] for j in range(m))
            for j in range(m):
                row = jnp.where(lane == k + j, q[i][j], row)
            col = jnp.where(in_sub, jnp.where(sub == k + i, -1.0, 0.0), a[:, k + i : k + i + 1])
            new = new - col * row
        a = new
    return a


def split(x):
    high = x.astype(jnp.bfloat16)
    return high, (x - high.astype(jnp.float32)).astype(jnp.bfloat16)


def product(a, b):
    out = jnp.dot(a[0], b[1], preferred_element_type=jnp.float32)
    out += jnp.dot(a[1], b[0], preferred_element_type=jnp.float32)
    return out + jnp.dot(a[0], b[0], preferred_element_type=jnp.float32)


def prepare_kernel(coords_ref, seg_ref, corner_ref, slot_ref, out_ref, *, held, holders, near):
    xi = lax.axis_index("corner")
    seg_i = lax.axis_index("y") * lax.axis_size("core") + lax.axis_index("core")
    cols = seg_ref.shape[1]
    seg = seg_ref[...]
    gram = lax.dot_general(seg, seg, (((0,), (0,)), ((), ())), preferred_element_type=jnp.float32)
    lane = lax.broadcasted_iota(jnp.int32, (1, cols), 1)
    rows = [jnp.zeros((1, cols), jnp.float32) for _ in range(near)]
    seen = []
    for t in range(coords_ref.shape[0]):
        local = jnp.clip(coords_ref[t, 2] - seg_i * (held * holders), 0, held * holders - 1)
        holder = local // held
        rank = jnp.int32(0)
        for other in seen:
            rank += (other == holder).astype(jnp.int32)
        rank = jnp.minimum(rank, CAP - 1)
        seen.append(holder)
        place = holder * CAP + rank
        shift = lax.rem(xi - holder // near + near, near)
        slot_ref[t] = shift * (near * CAP) + (holder % near) * CAP + rank
        for c in range(near):
            rows[c] = jnp.where(lane == place - c * near * CAP, (local % held).astype(jnp.float32), rows[c])
    corner = corner_ref[...].astype(jnp.float32)
    nseg = out_ref.shape[0] // near
    per = corner.shape[0] // nseg
    own = jnp.zeros((per, cols), jnp.float32)
    for s in range(nseg):
        own = jnp.where(seg_i == s, corner[s * per : (s + 1) * per], own)
    split_rows = 8 // near
    gram = gram.reshape(out_ref.shape[0], 8, cols)
    piece = jnp.zeros((out_ref.shape[0], split_rows, cols), jnp.float32)
    for c in range(near):
        piece = jnp.where(xi == c, gram[:, c * split_rows : (c + 1) * split_rows], piece)
    pad = jnp.zeros((8 - split_rows - 1 - per, cols), jnp.float32)
    for p in range(out_ref.shape[0]):
        out_ref[p] = jnp.concatenate([piece[p], rows[p % near], own, pad], axis=0)


def select_kernel(req_ref, *refs):
    hold = len(refs) // 2
    parts, outs = refs[:hold], refs[hold:]
    zl = lax.axis_index("zl")
    xi = lax.axis_index("corner")
    for offset in range(hold):
        residue = lax.rem(zl + offset, hold)
        for shift in range(hold):
            dest = lax.rem(xi + shift, hold)
            for rank in range(CAP):
                slot = residue * CAP + rank
                outs[shift][slot] = parts[offset][req_ref[dest, slot]]


def scale_kernel(corner_ref, out_ref):
    corner = corner_ref[...]
    n, cols = corner.shape
    wide = jnp.concatenate([corner, jnp.zeros((128 - n, cols), jnp.float32)], axis=0) if n < 128 else corner
    n = wide.shape[0]
    d = 1.0 / jnp.sum(wide * wide, axis=0, keepdims=True)
    scaled = wide * d
    eye = lax.broadcasted_iota(jnp.int32, (n, n), 0) == lax.broadcasted_iota(jnp.int32, (n, n), 1)
    inner = jnp.where(eye, 1.0, 0.0) + lax.dot_general(
        scaled, wide, (((1,), (1,)), ((), ())), precision=HIGH, preferred_element_type=jnp.float32
    )
    small = mm(invert_block(inner), scaled)
    low = lax.dot_general(
        scaled, small, (((0,), (0,)), ((), ())), precision=HIGH, preferred_element_type=jnp.float32
    )
    diag = lax.broadcasted_iota(jnp.int32, (cols, cols), 0) == lax.broadcasted_iota(jnp.int32, (cols, cols), 1)
    out_ref[...] = jnp.where(diag, d, 0.0) - low


def contract_kernel(seg_ids, corner_ids, keep_ids, send_ids, values_ref, *refs):
    seg_refs, (corner_ref, keep_ref, send_ref) = refs[:-3], refs[-3:]
    per = seg_refs[0].shape[0]
    step = pl.program_id(0)

    @pl.when(step == 0)
    def _():
        keep_ref[...] = jnp.zeros_like(keep_ref)
        send_ref[...] = jnp.zeros_like(send_ref)

    for g in range(values_ref.shape[0]):
        t = step * values_ref.shape[0] + g
        at = lax.rem(seg_ids[t], per)
        source = seg_ids[t] // per
        seg_rows = seg_refs[0][at]
        for k in range(1, len(seg_refs)):
            seg_rows = jnp.where(source == k, seg_refs[k][at], seg_rows)
        seg_rows = seg_rows.astype(jnp.float32)
        corner_rows = corner_ref[corner_ids[t]].astype(jnp.float32)
        khatri = jnp.concatenate(
            [(corner_rows[a : a + 1, :] * seg_rows).astype(jnp.bfloat16) for a in range(CBLK)], axis=0
        )
        part = jnp.dot(values_ref[g], khatri, preferred_element_type=jnp.float32)
        keep_ref[keep_ids[t]] += part
        send_ref[send_ids[t]] += part


def scaled_kernel(keep_ref, recv_ref, scale_ref, out_ref):
    scale = split(scale_ref[...])

    def block(i, carry):
        out_ref[i] = product(split(keep_ref[i] + recv_ref[i]), scale).astype(jnp.bfloat16)
        return carry

    lax.fori_loop(0, out_ref.shape[0], block, 0, unroll=4)


def inverse_kernel(seg_gram_ref, corner_ref, out_ref):
    cols = out_ref.shape[1]
    corner = corner_ref[...]
    low = corner.astype(jnp.bfloat16)
    corner_gram = lax.dot_general(low, low, (((0,), (0,)), ((), ())), preferred_element_type=jnp.float32)
    gram = seg_gram_ref[...].reshape(cols, cols) * corner_gram
    h = cols // 2
    a12 = gram[:h, h:]
    a21 = gram[h:, :h]
    p = invert_block(gram[:h, :h])
    w = mm(p, a12)
    v = mm(a21, p)
    q = invert_block(gram[h:, h:] - mm(a21, w))
    wq = mm(w, q)
    top = jnp.concatenate([p + mm(wq, v), -wq], axis=1)
    bottom = jnp.concatenate([-mm(q, v), q], axis=1)
    inverse = jnp.concatenate([top, bottom], axis=0)
    diag = lax.broadcasted_iota(jnp.int32, (cols, cols), 0) == lax.broadcasted_iota(jnp.int32, (cols, cols), 1)
    d = jnp.sum(corner * corner, axis=0, keepdims=True)
    out_ref[...] = mm(corner_gram + jnp.where(diag, d, 0.0), inverse)


def final_kernel(shares_ref, right_ref, out_ref):
    total = shares_ref[0].astype(jnp.float32)
    for i in range(1, shares_ref.shape[0]):
        total += shares_ref[i].astype(jnp.float32)
    out_ref[...] = product(split(total), split(right_ref[...]))


def call(kernel, name, out_shape, in_specs, out_specs, *operands, scratch=()):
    return pl.pallas_call(
        kernel,
        in_specs=in_specs,
        out_specs=out_specs,
        out_shape=out_shape,
        scratch_shapes=scratch,
        compiler_params=pltpu.CompilerParams(vmem_limit_bytes=32 << 20),
        cost_estimate=FREE,
        name=name,
    )(*operands)


def body(tile_values, tile_coords, tile_count, owner_map, corner_factor, seg_factor):
    tiles, net_rows, width = tile_values.shape
    cols = corner_factor.shape[1]
    seg_width = width // CBLK
    nz = lax.axis_size(NET)
    nx = lax.axis_size("corner")
    nseg = lax.axis_size(SEG)
    core = lax.axis_index("core")
    xi = lax.axis_index("corner")
    seg_i = lax.axis_index(SEG)
    per_corner = corner_factor.shape[0] // CBLK
    held = seg_factor.shape[0] // seg_width
    owners = lax.axis_size("y") * nx
    near = nz // nx
    f32 = functools.partial(jax.ShapeDtypeStruct, dtype=jnp.float32)
    smem = pl.BlockSpec(memory_space=pltpu.SMEM)
    vmem = pl.BlockSpec(memory_space=pltpu.VMEM)

    far = [
        (h * nx + x, (h + near * ((x + h) % nx)) % nz * nx + h // near)
        for h in range(nz)
        for x in range(nx)
    ]
    own_rows = lax.ppermute(seg_factor, NET + ("corner",), far)
    slot_of, packet = call(
        functools.partial(prepare_kernel, held=held, holders=nz, near=near),
        "prepare",
        [jax.ShapeDtypeStruct((tiles,), jnp.int32), f32((nseg * nx, 8, cols))],
        [smem, vmem, vmem],
        [smem, vmem],
        tile_coords,
        seg_factor,
        corner_factor,
    )
    packet = lax.all_to_all(packet, PLANE, 0, 0)
    own_rows, packet = lax.optimization_barrier((own_rows, packet))
    up = lax.ppermute(own_rows, NET, [((z + 1) % nz, z) for z in range(nz)])
    two = lax.ppermute(own_rows, NET, [((z + (2 if z % 2 else -2)) % nz, z) for z in range(nz)])
    down = lax.ppermute(own_rows, NET, [((z - 1) % nz, z) for z in range(nz)])
    packet = packet.reshape(nseg, nx, 8, cols)
    cut = 8 // nx
    corner_all = packet[:, :, cut + 1 : cut + 1 + corner_factor.shape[0] // nseg].reshape(-1, cols)
    request = lax.dynamic_index_in_dim(packet[:, :, cut, : near * CAP], seg_i, 0, keepdims=False)
    request = jnp.clip(request.astype(jnp.int32), 0, held - 1)
    chunk = jnp.sum(packet[:, :, :cut], axis=0).reshape(8, cols)
    chunk = jnp.sum(lax.all_to_all(jnp.broadcast_to(chunk[None], (near, 8, cols)), "zl", 0, 0), axis=0)
    scale = call(scale_kernel, "corner_scale", f32((cols, cols)), [vmem], vmem, corner_all)
    up, two, down, chunk, request, scale = lax.optimization_barrier((up, two, down, chunk, request, scale))
    chosen = call(
        select_kernel,
        "select_blocks",
        [jax.ShapeDtypeStruct((near * CAP, seg_width, cols), seg_factor.dtype)] * nx,
        [smem] + [vmem] * near,
        [vmem] * nx,
        request,
        *(v.reshape(held, seg_width, cols) for v in (own_rows, up, two, down)),
    )
    _, chunk = lax.optimization_barrier((chosen[1], chunk))
    blocks = [chosen[0]] + [
        lax.ppermute(chosen[k], "corner", [(x, (x + k) % nx) for x in range(nx)]) for k in range(1, nx)
    ]
    chunk = jnp.sum(lax.all_to_all(jnp.broadcast_to(chunk[None], (nz // near, 8, cols)), "zh", 0, 0), axis=0)

    corner_ids = jnp.clip(tile_coords[:, 0] - xi * per_corner, 0, per_corner - 1)
    match = tile_coords[:, 1][:, None] == owner_map[None, :]
    slot = jnp.sum(jnp.where(match, jnp.arange(owner_map.shape[0], dtype=jnp.int32)[None, :], 0), axis=1)
    place = (slot // (2 * nx)) * nx + slot % nx
    live = jnp.arange(tiles, dtype=jnp.int32) < tile_count[0]
    here = (slot // nx) % 2 == core
    keep_ids = jnp.where(live & here, place, owners)
    keep_ids, chunk = lax.optimization_barrier((keep_ids, chunk))
    seg_gram = lax.all_to_all(jnp.broadcast_to(chunk[None], (nseg * nx, 8, cols)), PLANE, 0, 0)
    send_ids = jnp.where(live & jnp.logical_not(here), place, owners)
    keep, send = pl.pallas_call(
        contract_kernel,
        grid_spec=pltpu.PrefetchScalarGridSpec(
            num_scalar_prefetch=4,
            grid=(tiles // GRP,),
            in_specs=[pl.BlockSpec((GRP, net_rows, width), lambda t, *_: (t, 0, 0))]
            + [vmem] * nx
            + [pl.BlockSpec((per_corner, CBLK, cols), lambda t, *_: (0, 0, 0))],
            out_specs=[pl.BlockSpec((owners + 1, net_rows, cols), lambda t, *_: (0, 0, 0))] * 2,
        ),
        out_shape=[f32((owners + 1, net_rows, cols))] * 2,
        compiler_params=pltpu.CompilerParams(vmem_limit_bytes=50 << 20),
        name="contract",
    )(
        slot_of,
        corner_ids,
        keep_ids,
        send_ids,
        tile_values,
        *blocks,
        corner_factor.reshape(per_corner, CBLK, cols),
    )
    send, seg_gram = lax.optimization_barrier((send, seg_gram))
    received = lax.ppermute(send, "core", [(0, 1), (1, 0)])
    solved = call(
        scaled_kernel,
        "apply_scale",
        jax.ShapeDtypeStruct((owners, net_rows, cols), jnp.bfloat16),
        [vmem] * 3,
        vmem,
        keep,
        received,
        scale,
    )
    shares = lax.all_to_all(solved, ("y", "corner"), 0, 0)
    right = call(inverse_kernel, "gram_inverse", f32((cols, cols)), [vmem] * 2, vmem, seg_gram, corner_all)
    return call(final_kernel, "final", f32((net_rows, cols)), [vmem] * 2, vmem, shares, right)


def solution(mesh):
    nz, seg, nx = mesh.devices.shape
    axes = Mesh(mesh.devices.reshape(nx, nz // nx, seg // 2, 2, nx), ALL)
    return jax.shard_map(
        body,
        mesh=axes,
        in_specs=(
            P(ALL, None, None),
            P(ALL, None),
            P(ALL),
            P(NET),
            P("corner", None),
            P(SEG + NET, None),
        ),
        out_specs=P(ALL, None),
        check_vma=False,
    )
```

```python
import jax
import jax.numpy as jnp
from jax import lax
from jax.experimental import pallas as pl
from jax.experimental.pallas import tpu as pltpu
from jax.sharding import Mesh, PartitionSpec as P

CBLK = 8
GRP = 8
PIVOTS = 4
NET = ("zh", "zl")
SEG = ("y", "core")
ALL = NET + SEG + ("corner",)
HIGH = lax.Precision.HIGHEST


def mm(a, b):
    return jnp.dot(a, b, precision=HIGH, preferred_element_type=jnp.float32)


def invert_pivot(p):
    m = len(p)
    if m == 2:
        inv = 1.0 / (p[0][0] * p[1][1] - p[0][1] * p[0][1])
        off = -p[0][1] * inv
        return [[p[1][1] * inv, off], [off, p[0][0] * inv]]
    h = m // 2
    r = range(h)
    ai = invert_pivot([row[:h] for row in p[:h]])
    b = [row[h:] for row in p[:h]]
    w = [[sum(ai[i][l] * b[l][j] for l in r) for j in r] for i in r]
    s = [[p[h + i][h + j] - sum(b[l][min(i, j)] * w[l][max(i, j)] for l in r) for j in r] for i in r]
    q = invert_pivot(s)
    wq = [[sum(w[i][l] * q[l][j] for l in r) for j in r] for i in r]
    top = [[ai[i][j] + sum(wq[i][l] * w[j][l] for l in r) for j in r] for i in r]
    return [top[i] + [-x for x in wq[i]] for i in r] + [[-wq[j][i] for j in r] + q[i] for i in r]


def invert_block(a):
    n = a.shape[0]
    m = PIVOTS
    lane = lax.broadcasted_iota(jnp.int32, (1, n), 1)
    sub = lax.broadcasted_iota(jnp.int32, (n, 1), 0)
    for k in range(0, n, m):
        rows = [a[k + i : k + i + 1, :] for i in range(m)]
        p = [[None] * m for _ in range(m)]
        for i in range(m):
            for j in range(i, m):
                p[i][j] = p[j][i] = jnp.broadcast_to(rows[i][:, k + j : k + j + 1], (1, n))
        q = invert_pivot(p)
        in_lane = (lane >= k) & (lane < k + m)
        in_sub = (sub >= k) & (sub < k + m)
        new = jnp.where(in_lane | in_sub, 0.0, a)
        for i in range(m):
            row = sum(q[i][j] * rows[j] for j in range(m))
            for j in range(m):
                row = jnp.where(lane == k + j, q[i][j], row)
            col = jnp.where(in_sub, jnp.where(sub == k + i, -1.0, 0.0), a[:, k + i : k + i + 1])
            new = new - col * row
        a = new
    return a


def inverse_kernel(packet_ref, out_ref):
    cols = out_ref.shape[1]
    packet = packet_ref[...]
    corner = packet[:, 8:, :].reshape(-1, cols).astype(jnp.bfloat16)
    gram = packet[:, :8, :].reshape(-1, cols) * lax.dot_general(
        corner, corner, (((0,), (0,)), ((), ())), preferred_element_type=jnp.float32
    )
    h = cols // 2
    a12 = gram[:h, h:]
    a21 = gram[h:, :h]
    p = invert_block(gram[:h, :h])
    w = mm(p, a12)
    v = mm(a21, p)
    q = invert_block(gram[h:, h:] - mm(a21, w))
    wq = mm(w, q)
    out_ref[:h, :h] = p + mm(wq, v)
    out_ref[:h, h:] = -wq
    out_ref[h:, :h] = -mm(q, v)
    out_ref[h:, h:] = q


def contract_kernel(seg_ids, corner_ids, keep_ids, send_ids, values_ref, *refs):
    seg_refs, (corner_ref, keep_ref, send_ref) = refs[:GRP], refs[GRP:]
    step = pl.program_id(0)
    owners = send_ref.shape[0]

    @pl.when(step == 0)
    def _():
        keep_ref[...] = jnp.zeros_like(keep_ref)
        send_ref[...] = jnp.zeros_like(send_ref)

    for g in range(GRP):
        t = step * GRP + g
        seg_rows = seg_refs[g][0].astype(jnp.float32)
        corner_rows = corner_ref[corner_ids[t]].astype(jnp.float32)
        khatri = jnp.concatenate(
            [(corner_rows[a : a + 1, :] * seg_rows).astype(jnp.bfloat16) for a in range(CBLK)], axis=0
        )
        part = jnp.dot(values_ref[g], khatri, preferred_element_type=jnp.float32)
        keep_ref[keep_ids[t]] += part
        slot = send_ids[t]
        send_ref[jnp.minimum(slot, owners - 1)] += jnp.where(slot < owners, part, 0.0)


def split(x):
    high = x.astype(jnp.bfloat16)
    return high, (x - high.astype(jnp.float32)).astype(jnp.bfloat16)


def whiten_kernel(keep_ref, recv_ref, inv_ref, out_ref):
    inv_high, inv_low = split(inv_ref[...])

    def block(i, carry):
        rows_high, rows_low = split(keep_ref[i] + recv_ref[i])
        out = jnp.dot(rows_high, inv_low, preferred_element_type=jnp.float32)
        out += jnp.dot(rows_low, inv_high, preferred_element_type=jnp.float32)
        out += jnp.dot(rows_high, inv_high, preferred_element_type=jnp.float32)
        out_ref[i] = out.astype(jnp.bfloat16)
        return carry

    lax.fori_loop(0, out_ref.shape[0], block, 0, unroll=True)


def body(tile_values, tile_coords, tile_count, owner_map, corner_factor, seg_factor):
    tiles, net_rows, width = tile_values.shape
    cols = corner_factor.shape[1]
    seg_width = width // CBLK
    nz = lax.axis_size(NET)
    ny = lax.axis_size("y")
    nx = lax.axis_size("corner")
    core = lax.axis_index("core")
    xi = lax.axis_index("corner")
    seg_i = lax.axis_index("y") * lax.axis_size("core") + core
    per_corner = corner_factor.shape[0] // CBLK
    held = seg_factor.shape[0] // seg_width
    owners = ny * nx

    gathered = lax.all_gather(seg_factor, NET, axis=0, tiled=True)

    seg_part = lax.dot_general(
        seg_factor, seg_factor, (((0,), (0,)), ((), ())), preferred_element_type=jnp.float32
    )
    nseg = ny * lax.axis_size("core")
    mine = lax.dynamic_index_in_dim(seg_part.reshape(nseg, nx, -1, cols), xi, 1, keepdims=False)
    chunk = jnp.sum(lax.all_to_all(mine, SEG, 0, 0), axis=0)
    for axis in NET:
        spread = jnp.broadcast_to(chunk[None], (lax.axis_size(axis),) + chunk.shape)
        chunk = jnp.sum(lax.all_to_all(spread, axis, 0, 0), axis=0)
    crows = corner_factor.shape[0] // nseg
    own = lax.dynamic_slice_in_dim(corner_factor, seg_i * crows, crows, 0).astype(jnp.float32)
    packet = jnp.concatenate([chunk, jnp.pad(own, ((0, 8 - crows), (0, 0)))], axis=0)
    packet = jnp.broadcast_to(packet[None], (nseg * nx,) + packet.shape)
    packet = lax.all_to_all(packet, SEG + ("corner",), 0, 0)
    inverse = pl.pallas_call(
        inverse_kernel,
        out_shape=jax.ShapeDtypeStruct((cols, cols), jnp.float32),
        compiler_params=pltpu.CompilerParams(vmem_limit_bytes=32 << 20),
        name="gram_inverse",
    )(packet)
    gathered, inverse = lax.optimization_barrier((gathered, inverse))

    corner_ids = jnp.clip(tile_coords[:, 0] - xi * per_corner, 0, per_corner - 1)
    seg_ids = jnp.clip(tile_coords[:, 2] - seg_i * (held * nz), 0, held * nz - 1)
    match = tile_coords[:, 1][:, None] == owner_map[None, :]
    slot = jnp.sum(jnp.where(match, jnp.arange(owner_map.shape[0], dtype=jnp.int32)[None, :], 0), axis=1)
    place = (slot // (2 * nx)) * nx + slot % nx
    live = jnp.arange(tiles, dtype=jnp.int32) < tile_count[0]
    here = (slot // nx) % 2 == core
    keep_ids = jnp.where(live & here, place, owners)
    send_ids = jnp.where(live & jnp.logical_not(here), place, owners)

    blocks = gathered.reshape(-1, seg_width, cols)

    def seg_spec(g):
        return pl.BlockSpec((1, seg_width, cols), lambda t, ids, *_: (ids[t * GRP + g], 0, 0))

    keep, send = pl.pallas_call(
        contract_kernel,
        grid_spec=pltpu.PrefetchScalarGridSpec(
            num_scalar_prefetch=4,
            grid=(tiles // GRP,),
            in_specs=[
                pl.BlockSpec((GRP, net_rows, width), lambda t, *_: (t, 0, 0)),
                *[seg_spec(g) for g in range(GRP)],
                pl.BlockSpec((per_corner, CBLK, cols), lambda t, *_: (0, 0, 0)),
            ],
            out_specs=[
                pl.BlockSpec((owners + 1, net_rows, cols), lambda t, *_: (0, 0, 0)),
                pl.BlockSpec((owners, net_rows, cols), lambda t, *_: (0, 0, 0)),
            ],
        ),
        out_shape=[
            jax.ShapeDtypeStruct((owners + 1, net_rows, cols), jnp.float32),
            jax.ShapeDtypeStruct((owners, net_rows, cols), jnp.float32),
        ],
        compiler_params=pltpu.CompilerParams(vmem_limit_bytes=48 << 20),
        name="contract",
    )(
        seg_ids,
        corner_ids,
        keep_ids,
        send_ids,
        tile_values,
        *[blocks] * GRP,
        corner_factor.reshape(per_corner, CBLK, cols),
    )
    received = lax.ppermute(send, "core", [(0, 1), (1, 0)])
    solved = pl.pallas_call(
        whiten_kernel,
        out_shape=jax.ShapeDtypeStruct((owners, net_rows, cols), jnp.bfloat16),
        compiler_params=pltpu.CompilerParams(vmem_limit_bytes=32 << 20),
        name="apply_inverse",
    )(keep, received, inverse)
    shares = lax.all_to_all(solved, ("y", "corner"), 0, 0)
    return jnp.sum(shares.astype(jnp.float32), axis=0)


def solution(mesh):
    nz, seg, nx = mesh.devices.shape
    split = Mesh(mesh.devices.reshape(4, nz // 4, seg // 2, 2, nx), ALL)
    return jax.shard_map(
        body,
        mesh=split,
        in_specs=(
            P(ALL, None, None),
            P(ALL, None),
            P(ALL),
            P(NET),
            P("corner", None),
            P(SEG + NET, None),
        ),
        out_specs=P(ALL, None),
        check_vma=False,
    )
```

```python
import jax
import jax.numpy as jnp
from jax import lax
from jax.experimental import pallas as pl
from jax.experimental.pallas import tpu as pltpu
from jax.sharding import Mesh, PartitionSpec as P

CBLK = 8
GRP = 8
PIVOTS = 4
NET = ("zh", "zl")
SEG = ("y", "core")
ALL = NET + SEG + ("corner",)
HIGH = lax.Precision.HIGHEST


def mm(a, b):
    return jnp.dot(a, b, precision=HIGH, preferred_element_type=jnp.float32)


def invert_pivot(p):
    m = len(p)
    if m == 2:
        inv = 1.0 / (p[0][0] * p[1][1] - p[0][1] * p[0][1])
        off = -p[0][1] * inv
        return [[p[1][1] * inv, off], [off, p[0][0] * inv]]
    h = m // 2
    r = range(h)
    ai = invert_pivot([row[:h] for row in p[:h]])
    b = [row[h:] for row in p[:h]]
    w = [[sum(ai[i][l] * b[l][j] for l in r) for j in r] for i in r]
    s = [[p[h + i][h + j] - sum(b[l][min(i, j)] * w[l][max(i, j)] for l in r) for j in r] for i in r]
    q = invert_pivot(s)
    wq = [[sum(w[i][l] * q[l][j] for l in r) for j in r] for i in r]
    top = [[ai[i][j] + sum(wq[i][l] * w[j][l] for l in r) for j in r] for i in r]
    return [top[i] + [-x for x in wq[i]] for i in r] + [[-wq[j][i] for j in r] + q[i] for i in r]


def invert_block(a):
    n = a.shape[0]
    m = PIVOTS
    lane = lax.broadcasted_iota(jnp.int32, (1, n), 1)
    sub = lax.broadcasted_iota(jnp.int32, (n, 1), 0)
    for k in range(0, n, m):
        rows = [a[k + i : k + i + 1, :] for i in range(m)]
        p = [[None] * m for _ in range(m)]
        for i in range(m):
            for j in range(i, m):
                p[i][j] = p[j][i] = jnp.broadcast_to(rows[i][:, k + j : k + j + 1], (1, n))
        q = invert_pivot(p)
        in_lane = (lane >= k) & (lane < k + m)
        in_sub = (sub >= k) & (sub < k + m)
        new = jnp.where(in_lane | in_sub, 0.0, a)
        for i in range(m):
            row = sum(q[i][j] * rows[j] for j in range(m))
            for j in range(m):
                row = jnp.where(lane == k + j, q[i][j], row)
            col = jnp.where(in_sub, jnp.where(sub == k + i, -1.0, 0.0), a[:, k + i : k + i + 1])
            new = new - col * row
        a = new
    return a


def inverse_kernel(packet_ref, out_ref):
    cols = out_ref.shape[1]
    packet = packet_ref[...]
    corner = packet[:, 8:, :].reshape(-1, cols).astype(jnp.bfloat16)
    gram = packet[:, :8, :].reshape(-1, cols) * lax.dot_general(
        corner, corner, (((0,), (0,)), ((), ())), preferred_element_type=jnp.float32
    )
    h = cols // 2
    a12 = gram[:h, h:]
    a21 = gram[h:, :h]
    p = invert_block(gram[:h, :h])
    w = mm(p, a12)
    v = mm(a21, p)
    q = invert_block(gram[h:, h:] - mm(a21, w))
    wq = mm(w, q)
    out_ref[:h, :h] = p + mm(wq, v)
    out_ref[:h, h:] = -wq
    out_ref[h:, :h] = -mm(q, v)
    out_ref[h:, h:] = q


def contract_kernel(seg_ids, corner_ids, keep_ids, send_ids, values_ref, *refs):
    seg_refs, (corner_ref, keep_ref, send_ref) = refs[:GRP], refs[GRP:]
    step = pl.program_id(0)
    owners = send_ref.shape[0]

    @pl.when(step == 0)
    def _():
        keep_ref[...] = jnp.zeros_like(keep_ref)
        send_ref[...] = jnp.zeros_like(send_ref)

    for g in range(GRP):
        t = step * GRP + g
        seg_rows = seg_refs[g][0]
        corner_rows = corner_ref[corner_ids[t]]
        khatri = jnp.concatenate(
            [corner_rows[a : a + 1, :] * seg_rows for a in range(CBLK)], axis=0
        )
        part = jnp.dot(values_ref[g], khatri, preferred_element_type=jnp.float32)
        keep_ref[keep_ids[t]] += part
        slot = send_ids[t]
        send_ref[jnp.minimum(slot, owners - 1)] += jnp.where(slot < owners, part, 0.0)


def split(x):
    high = x.astype(jnp.bfloat16)
    return high, (x - high.astype(jnp.float32)).astype(jnp.bfloat16)


def whiten_kernel(keep_ref, recv_ref, inv_ref, out_ref):
    inv_high, inv_low = split(inv_ref[...])

    def block(i, carry):
        rows_high, rows_low = split(keep_ref[i] + recv_ref[i])
        out = jnp.dot(rows_high, inv_low, preferred_element_type=jnp.float32)
        out += jnp.dot(rows_low, inv_high, preferred_element_type=jnp.float32)
        out += jnp.dot(rows_high, inv_high, preferred_element_type=jnp.float32)
        out_ref[i] = out.astype(jnp.bfloat16)
        return carry

    lax.fori_loop(0, out_ref.shape[0], block, 0, unroll=True)


def body(tile_values, tile_coords, tile_count, owner_map, corner_factor, seg_factor):
    tiles, net_rows, width = tile_values.shape
    cols = corner_factor.shape[1]
    seg_width = width // CBLK
    nz = lax.axis_size(NET)
    ny = lax.axis_size("y")
    nx = lax.axis_size("corner")
    core = lax.axis_index("core")
    xi = lax.axis_index("corner")
    seg_i = lax.axis_index("y") * lax.axis_size("core") + core
    per_corner = corner_factor.shape[0] // CBLK
    held = seg_factor.shape[0] // seg_width
    owners = ny * nx

    gathered = lax.all_gather(seg_factor, NET, axis=0, tiled=True)

    seg_part = lax.dot_general(
        seg_factor, seg_factor, (((0,), (0,)), ((), ())), preferred_element_type=jnp.float32
    )
    nseg = ny * lax.axis_size("core")
    mine = lax.dynamic_index_in_dim(seg_part.reshape(nseg, nx, -1, cols), xi, 1, keepdims=False)
    chunk = jnp.sum(lax.all_to_all(mine, SEG, 0, 0), axis=0)
    for axis in NET:
        spread = jnp.broadcast_to(chunk[None], (lax.axis_size(axis),) + chunk.shape)
        chunk = jnp.sum(lax.all_to_all(spread, axis, 0, 0), axis=0)
    crows = corner_factor.shape[0] // nseg
    own = lax.dynamic_slice_in_dim(corner_factor, seg_i * crows, crows, 0).astype(jnp.float32)
    packet = jnp.concatenate([chunk, jnp.pad(own, ((0, 8 - crows), (0, 0)))], axis=0)
    packet = jnp.broadcast_to(packet[None], (nseg * nx,) + packet.shape)
    packet = lax.all_to_all(packet, SEG + ("corner",), 0, 0)
    inverse = pl.pallas_call(
        inverse_kernel,
        out_shape=jax.ShapeDtypeStruct((cols, cols), jnp.float32),
        compiler_params=pltpu.CompilerParams(vmem_limit_bytes=32 << 20),
        name="gram_inverse",
    )(packet)
    gathered, inverse = lax.optimization_barrier((gathered, inverse))

    corner_ids = jnp.clip(tile_coords[:, 0] - xi * per_corner, 0, per_corner - 1)
    seg_ids = jnp.clip(tile_coords[:, 2] - seg_i * (held * nz), 0, held * nz - 1)
    match = tile_coords[:, 1][:, None] == owner_map[None, :]
    slot = jnp.sum(jnp.where(match, jnp.arange(owner_map.shape[0], dtype=jnp.int32)[None, :], 0), axis=1)
    place = (slot // (2 * nx)) * nx + slot % nx
    live = jnp.arange(tiles, dtype=jnp.int32) < tile_count[0]
    here = (slot // nx) % 2 == core
    keep_ids = jnp.where(live & here, place, owners)
    send_ids = jnp.where(live & jnp.logical_not(here), place, owners)

    blocks = gathered.reshape(-1, seg_width, cols)

    def seg_spec(g):
        return pl.BlockSpec((1, seg_width, cols), lambda t, ids, *_: (ids[t * GRP + g], 0, 0))

    keep, send = pl.pallas_call(
        contract_kernel,
        grid_spec=pltpu.PrefetchScalarGridSpec(
            num_scalar_prefetch=4,
            grid=(tiles // GRP,),
            in_specs=[
                pl.BlockSpec((GRP, net_rows, width), lambda t, *_: (t, 0, 0)),
                *[seg_spec(g) for g in range(GRP)],
                pl.BlockSpec((per_corner, CBLK, cols), lambda t, *_: (0, 0, 0)),
            ],
            out_specs=[
                pl.BlockSpec((owners + 1, net_rows, cols), lambda t, *_: (0, 0, 0)),
                pl.BlockSpec((owners, net_rows, cols), lambda t, *_: (0, 0, 0)),
            ],
        ),
        out_shape=[
            jax.ShapeDtypeStruct((owners + 1, net_rows, cols), jnp.float32),
            jax.ShapeDtypeStruct((owners, net_rows, cols), jnp.float32),
        ],
        compiler_params=pltpu.CompilerParams(vmem_limit_bytes=48 << 20),
        name="contract",
    )(
        seg_ids,
        corner_ids,
        keep_ids,
        send_ids,
        tile_values,
        *[blocks] * GRP,
        corner_factor.reshape(per_corner, CBLK, cols),
    )
    received = lax.ppermute(send, "core", [(0, 1), (1, 0)])
    solved = pl.pallas_call(
        whiten_kernel,
        out_shape=jax.ShapeDtypeStruct((owners, net_rows, cols), jnp.bfloat16),
        compiler_params=pltpu.CompilerParams(vmem_limit_bytes=32 << 20),
        name="apply_inverse",
    )(keep, received, inverse)
    shares = lax.all_to_all(solved, ("y", "corner"), 0, 0)
    return jnp.sum(shares.astype(jnp.float32), axis=0)


def solution(mesh):
    nz, seg, nx = mesh.devices.shape
    split = Mesh(mesh.devices.reshape(4, nz // 4, seg // 2, 2, nx), ALL)
    return jax.shard_map(
        body,
        mesh=split,
        in_specs=(
            P(ALL, None, None),
            P(ALL, None),
            P(ALL),
            P(NET),
            P("corner", None),
            P(SEG + NET, None),
        ),
        out_specs=P(ALL, None),
        check_vma=False,
    )
```
